128 devices in a mesh: shard: 8 (over y_lo, z), ctx: 4 (over x), tp: 4 (over y_hi, core).
Axes of the slice: x: 4, y: 4 (y_hi: 2, y_lo: 2; y = y_hi * 2 + y_lo), z: 4, core: 2. Of those that a mesh axis runs over, the one named last changes fastest.
Arguments:
- tokens: bfloat16 [16, 1376, 1024], P('shard', 'ctx'), may hold values from -6 to 6
- cotangent: bfloat16 [16, 1376, 1024], P('shard', 'ctx'), may hold values from -6 to 6
- slot_live: int32 [16], P('shard'), may hold values from 0 to 1, as said below
- block_rows: int32 [16, 4], P('shard'), may hold values from 1 to 344, 1370 in all within a row
- ln1_gain: float32 [1024], replicated, may hold values from 0.1 to 1.9
- ln1_bias: float32 [1024], replicated, may hold values from -3 to 3
- w_qkv: bfloat16 [1024, 3, 1024], P(('shard', 'ctx'), None, 'tp'), may hold values from -0.1875 to 0.1875
- b_qv: float32 [2, 1024], P(None, 'tp'), may hold values from -3 to 3
- w_proj: bfloat16 [1024, 1024], P(('shard', 'ctx'), 'tp'), may hold values from -1.5 to 1.5
- b_proj: float32 [1024], replicated, may hold values from -3 to 3
- scale_attn: float32 [1024], replicated, may hold values from 0.1 to 1.9
- ln2_gain: float32 [1024], replicated, may hold values from 0.1 to 1.9
- ln2_bias: float32 [1024], replicated, may hold values from -3 to 3
- w_up: bfloat16 [1024, 4096], P(('shard', 'ctx'), 'tp'), may hold values from -0.1875 to 0.1875
- b_up: float32 [4096], P('tp'), may hold values from -3 to 3
- w_down: bfloat16 [1024, 4096], P(('shard', 'ctx'), 'tp'), may hold values from -0.09375 to 0.09375
- b_down: float32 [1024], replicated, may hold values from -3 to 3
- scale_mlp: float32 [1024], replicated, may hold values from 0.1 to 1.9
Outputs:
- result: bfloat16 [16, 1376, 1024], P('shard', 'ctx')
- d_tokens: float32 [16, 1376, 1024], P('shard', 'ctx')
- d_ln1_gain: float32 [1024], replicated
- d_ln1_bias: float32 [1024], replicated
- d_w_qkv: float32 [1024, 3, 1024], P(('shard', 'ctx'), None, 'tp')
- d_b_qv: float32 [2, 1024], P(None, 'tp')
- d_w_proj: float32 [1024, 1024], P(('shard', 'ctx'), 'tp')
- d_b_proj: float32 [1024], replicated
- d_scale_attn: float32 [1024], replicated
- d_ln2_gain: float32 [1024], replicated
- d_ln2_bias: float32 [1024], replicated
- d_w_up: float32 [1024, 4096], P(('shard', 'ctx'), 'tp')
- d_b_up: float32 [4096], P('tp')
- d_w_down: float32 [1024, 4096], P(('shard', 'ctx'), 'tp')
- d_b_down: float32 [1024], replicated
- d_scale_mlp: float32 [1024], replicated
The draws below stay inside these ranges and needn't reach their ends.
Inputs may be any that keep to these rules, and one draw needn't show every extreme that they name: `slot_live`: each index of shard owns 2 consecutive slots, the first of which always holds an image; exactly 13 slots hold one. `block_rows`: each slot's row of 4 entries sums to 1370.
All inputs are finite; a program needn't handle non-finite values.
Results may differ from the reference program's by a relative error of at most 0.02.
Values may be sent and summed in bfloat16 or wider, within the bound.
No kernel may reach another device: no remote copies, remote signals or barrier semaphores. Data moves between devices by JAX's collectives and lax.ppermute only.
A program may use at most 128 MiB of HBM per device.

```python
import math
import jax
import jax.numpy as jnp
import numpy as np
from jax import lax

D = 1024
HEADS = 16
FF = 4096
HEAD_DIM = 64
LEN = 1370
SLOT_DEV = 2
CT = 344
ROWS = 1376
SLOTS = 16
IMAGES = 13
N_SHARD = 8
N_CTX = 4


def draw_slot_live(key, part):
    dead_count = SLOTS - IMAGES
    spare_slots = N_SHARD * (SLOT_DEV - 1)
    ranking = jax.random.permutation(key, spare_slots)
    later_live = (ranking >= dead_count).astype(jnp.int32).reshape(N_SHARD, SLOT_DEV - 1)
    first_live = jnp.ones((N_SHARD, 1), jnp.int32)
    return jnp.concatenate([first_live, later_live], axis=1).reshape(SLOTS)


def block_levels(stream_key, extent, cuts, least, top_value):
    factor_of, own = 1.0, jax.random.fold_in(stream_key, 6)
    for dim, blocks in cuts:
        draws = jnp.exp(jax.random.uniform(jax.random.fold_in(own, dim), (blocks,), jnp.float32, least / len(cuts), top_value / len(cuts)))
        factor_of = factor_of * jnp.repeat(draws, extent[dim] // blocks).reshape([-1 if axis == dim else 1 for axis in range(len(extent))])
    return factor_of


def length_profile(number_of, total, reach, lean):
    weights = [(1 << 20) // math.isqrt(rank ** lean) + 1 for rank in range(2, number_of + 1)]
    rest, given = total - reach - (number_of - 1), [1] * (number_of - 1)
    while rest > 0:
        movable = [i for i in range(number_of - 1) if given[i] < reach]
        whole, budget = sum([weights[i] for i in movable]), rest
        for i in movable:
            more = min(reach - given[i], max(1, budget * weights[i] // whole), rest)
            given[i] = given[i] + more
            rest = rest - more
    return np.array([reach] + given)


def ragged_sizes(stream_key, number_of, total, most, skew):
    if number_of == 2:
        one = jax.random.randint(stream_key, (), max(1, total - most), min(most, total - 1) + 1)
        return jnp.stack([one, total - one])
    sizes = jnp.asarray(length_profile(number_of, total, most, skew), jnp.int32)
    couples = (number_of - 1) // 2
    donor, receiver = sizes[1:1 + 2 * couples:2], sizes[2:2 + 2 * couples:2]
    room = jnp.minimum(donor - 1, most - receiver)
    moved = jax.random.randint(jax.random.fold_in(stream_key, 1), (couples,), 0, 1 << 20) % (room + 1)
    sizes = sizes.at[1:1 + 2 * couples:2].set(donor - moved).at[2:2 + 2 * couples:2].set(receiver + moved)
    return sizes[jax.random.permutation(jax.random.fold_in(stream_key, 2), number_of)]


def gaussian(key, extent, deviation, bound, shards=(), kind=jnp.bfloat16):
    entries = jax.random.normal(key, extent, jnp.float32) * deviation
    if len(shards) > 0:
        entries = block_levels(key, extent, shards, -0.22, 0.18) * entries
    return jnp.clip(entries, min=-bound, max=bound).astype(kind)


def setup_inputs(seed: int = 0) -> dict:
    arg_keys = jax.random.split(jax.random.key(seed), 19)
    return {
        "tokens": gaussian(arg_keys[0], (SLOTS, ROWS, D), 1.0, 6.0, ((0, 8), (1, 4))),
        "cotangent": gaussian(arg_keys[1], (SLOTS, ROWS, D), 1.0, 6.0, ((0, 8), (1, 4))),
        "slot_live": draw_slot_live(jax.random.fold_in(arg_keys[18], 71), 0),
        "block_rows": jax.vmap(lambda own: ragged_sizes(own, N_CTX, LEN, CT, 1))(jax.random.split(arg_keys[3], SLOTS)).reshape((SLOTS, N_CTX)).astype(jnp.int32),
        "ln1_gain": jnp.clip(1.0 + 0.18 * jax.random.normal(arg_keys[4], (D,), jnp.float32), 0.1, 1.9),
        "ln1_bias": gaussian(arg_keys[5], (D,), 0.3, 3.0, (), jnp.float32),
        "w_qkv": gaussian(arg_keys[6], (D, 3, D), D ** -0.5, 0.1875, ((0, 32), (2, 4))),
        "b_qv": gaussian(arg_keys[7], (2, D), 0.5, 3.0, ((1, 4),), jnp.float32),
        "w_proj": gaussian(arg_keys[8], (D, D), (D // 64) ** -0.5, 1.5, ((0, 32), (1, 4))),
        "b_proj": gaussian(arg_keys[9], (D,), 0.3, 3.0, (), jnp.float32),
        "scale_attn": jnp.clip(1.0 + 0.18 * jax.random.normal(arg_keys[10], (D,), jnp.float32), 0.1, 1.9),
        "ln2_gain": jnp.clip(1.0 + 0.18 * jax.random.normal(arg_keys[11], (D,), jnp.float32), 0.1, 1.9),
        "ln2_bias": gaussian(arg_keys[12], (D,), 0.3, 3.0, (), jnp.float32),
        "w_up": gaussian(arg_keys[13], (D, FF), D ** -0.5, 0.1875, ((0, 32), (1, 4))),
        "b_up": gaussian(arg_keys[14], (FF,), 0.5, 3.0, ((0, 4),), jnp.float32),
        "w_down": gaussian(arg_keys[15], (D, FF), FF ** -0.5, 0.09375, ((0, 32), (1, 4))),
        "b_down": gaussian(arg_keys[16], (D,), 0.3, 3.0, (), jnp.float32),
        "scale_mlp": jnp.clip(1.0 + 0.18 * jax.random.normal(arg_keys[17], (D,), jnp.float32), 0.1, 1.9),
    }


@jax.custom_vjp
def low(v):
    return lax.optimization_barrier(v.astype(jnp.bfloat16)).astype(jnp.float32)

@jax.custom_vjp
def low_back(v):
    return v

def low_keep(v):
    return (low(v), None)

def low_pass(kept, grad):
    return (grad,)

def back_keep(v):
    return (v, None)

def back_low(kept, grad):
    return (low(grad),)
low.defvjp(low_keep, low_pass)
low_back.defvjp(back_keep, back_low)
EPSILON = 1e-06
HIGHEST = lax.Precision.HIGHEST
MASKED = -1e+30

def normalize(values, gain, offset):
    average = lax.optimization_barrier(jnp.mean(values, axis=-1, keepdims=True))
    centered = values - average
    variance = lax.optimization_barrier(jnp.mean(centered * centered, axis=-1, keepdims=True))
    return centered * lax.rsqrt(variance + EPSILON) * gain + offset

def forward(params, image_rows, row_mask):
    ln1_gain, ln1_bias, w_qkv, b_qv, w_proj, b_proj, scale_attn, ln2_gain, ln2_bias, w_up, b_up, w_down, b_down, scale_mlp = params
    length = image_rows.shape[0]
    normed = low(normalize(image_rows, ln1_gain, ln1_bias))
    mixed_qkv = jnp.einsum('rd,dcf->rcf', normed, w_qkv, precision=HIGHEST)
    shifts = jnp.stack([b_qv[0], jnp.zeros_like(b_qv[0]), b_qv[1]])
    mixed_qkv = low(low_back(mixed_qkv + shifts[None]))
    split_heads = mixed_qkv.reshape(length, 3, HEADS, HEAD_DIM)
    queries = split_heads[:, 0]
    key_rows = split_heads[:, 1]
    value_rows = split_heads[:, 2]
    scores = jnp.einsum('qhe,khe->hqk', queries, key_rows, precision=HIGHEST) * HEAD_DIM ** (-0.5)
    scores = low_back(jnp.where(row_mask[None, None, :] > 0, scores, MASKED))
    soft_weights = low(jax.nn.softmax(scores, axis=-1))
    attended = jnp.einsum('hqk,khe->qhe', soft_weights, value_rows, precision=HIGHEST)
    attended = low(low_back(attended.reshape(length, HEADS * HEAD_DIM)))
    branch_attn = low_back(jnp.dot(attended, w_proj.T, precision=HIGHEST) + b_proj)
    middle = image_rows + scale_attn * branch_attn
    second = low(normalize(middle, ln2_gain, ln2_bias))
    hidden = low_back(jnp.dot(second, w_up, precision=HIGHEST) + b_up)
    active = low(jax.nn.gelu(hidden, approximate=False))
    branch_mlp = low_back(jnp.dot(active, w_down.T, precision=HIGHEST) + b_down)
    return row_mask[:, None] * (middle + scale_mlp * branch_mlp)

def reference(tokens, cotangent, slot_live, block_rows, ln1_gain, ln1_bias, w_qkv, b_qv, w_proj, b_proj, scale_attn, ln2_gain, ln2_bias, w_up, b_up, w_down, b_down, scale_mlp):
    params = tuple((member.astype(jnp.float32) for member in (ln1_gain, ln1_bias, w_qkv, b_qv, w_proj, b_proj, scale_attn, ln2_gain, ln2_bias, w_up, b_up, w_down, b_down, scale_mlp)))
    positions = jnp.arange(ROWS).astype(jnp.int32)
    owners = (positions // CT).astype(jnp.int32)
    within = positions % CT

    def one_image(totals, inputs):
        image_rows, grad_rows, live_flag, counts = inputs
        is_valid = (within < counts[owners]) & (live_flag > 0)
        row_mask = is_valid.astype(jnp.float32)

        def apply_layer(weight_set, source):
            return forward(weight_set, source, row_mask)
        output_rows, pullback = jax.vjp(apply_layer, params, image_rows.astype(jnp.float32))
        grad_params, grad_image = pullback(grad_rows.astype(jnp.float32))
        totals = jax.tree.map(lambda total, extra: total + extra, totals, grad_params)
        return (totals, (output_rows.astype(jnp.bfloat16), grad_image))
    initial = jax.tree.map(jnp.zeros_like, params)
    totals, (outputs, input_grads) = lax.scan(one_image, initial, (tokens, cotangent, slot_live, block_rows))
    return (outputs, input_grads, totals[0], totals[1], totals[2], totals[3], totals[4], totals[5], totals[6], totals[7], totals[8], totals[9], totals[10], totals[11], totals[12], totals[13])
```

```python
import jax
import jax.numpy as jnp
from jax import lax
from jax.experimental import pallas as pl
from jax.experimental.pallas import tpu as pltpu
from jax.sharding import PartitionSpec as P

HEAD_DIM = 64
EPSILON = 1e-06
MASKED = -1e30
RING = 4
BF16 = jnp.bfloat16
F32 = jnp.float32

DIM = {"y": 0, "z": 1, "x": 2}


def shift_pairs(axis, step):
    if axis == "x":
        return "ctx", [(i, (i + step) % RING) for i in range(RING)]
    if axis == "z":
        return "shard", [
            (low * RING + z, low * RING + (z + step) % RING) for low in range(2) for z in range(RING)
        ]
    pairs = []
    for y in range(RING):
        for z in range(RING):
            for core in range(2):
                ends = [
                    ((at % 2) * RING + z) * 4 + (at // 2) * 2 + core for at in (y, (y + step) % RING)
                ]
                pairs.append(tuple(ends))
    return ("shard", "tp"), pairs


def shift(value, axis, step):
    names, pairs = shift_pairs(axis, step)
    return lax.ppermute(value, names, pairs)


def swap(value, bit):
    return lax.ppermute(value, "tp", [(i, i ^ bit) for i in range(4)])


def positions():
    shard, tp = lax.axis_index("shard"), lax.axis_index("tp")
    return {
        "x": lax.axis_index("ctx"),
        "z": shard % RING,
        "y": (tp // 2) * 2 + shard // RING,
    }


def assemble(parts, at, dim):
    shape = list(parts[0].shape)
    shape[dim] *= RING
    out = jnp.zeros(shape, parts[0].dtype)
    size = parts[0].shape[dim]
    for step, part in enumerate(parts):
        out = lax.dynamic_update_slice_in_dim(out, part, ((at - step) % RING) * size, dim)
    return out


def gather_axis(value, axis, at, dim):
    return assemble([value] + [shift(value, axis, s) for s in range(1, RING)], at, dim)


def gather(chunk, order, at):
    value = chunk[None, None, None]
    for axis in order:
        value = gather_axis(value, axis, at[axis], DIM[axis])
    return value.reshape(2, RING * RING * 2 * chunk.shape[0], chunk.shape[1])


def scatter_sum(halves, order, at):
    rows, columns = halves[0].shape
    value = jnp.stack(halves).reshape(RING, RING, RING, rows // 32, columns)
    for place, axis in enumerate(order):
        dim = DIM[axis]
        total = lax.dynamic_slice_in_dim(value, at[axis], 1, dim).astype(F32)
        for step in range(1, RING):
            block = lax.dynamic_slice_in_dim(value, (at[axis] + step) % RING, 1, dim)
            total = total + shift(block, axis, step).astype(F32)
        value = total if place == len(order) - 1 else total.astype(BF16)
    return value.reshape(rows // 32, columns)


def sum_everywhere(vector, at):
    for axis in ("x", "z", "y"):
        vector = jnp.sum(gather_axis(vector[None], axis, at[axis], 0), axis=0)
    return vector


def exchange(blocks, at):
    parts = [lax.dynamic_slice_in_dim(blocks, at, 1, 0)]
    for step in range(1, RING):
        parts.append(shift(lax.dynamic_slice_in_dim(blocks, (at + step) % RING, 1, 0), "x", step))
    return assemble(parts, at, 0)


def layer_stats(values):
    average = jnp.mean(values, axis=-1, keepdims=True)
    centered = values - average
    variance = jnp.mean(centered * centered, axis=-1, keepdims=True)
    inverse = lax.rsqrt(variance + EPSILON)
    return (centered * inverse, inverse)


def norm_back(grad_hat, normal_hat, inverse):
    first_term = jnp.mean(grad_hat, axis=-1, keepdims=True)
    second_term = jnp.mean(grad_hat * normal_hat, axis=-1, keepdims=True)
    return inverse * (grad_hat - first_term - normal_hat * second_term)


def dot(left, right, left_dim, right_dim):
    return lax.dot_general(
        left, right, (((left_dim,), (right_dim,)), ((), ())), preferred_element_type=F32
    )


def pair_sum(part):
    low = part.astype(BF16)
    return low.astype(F32) + swap(low, 1).astype(F32)


def attention_forward(q_ref, k_ref, v_ref, bias_ref, out_ref, log_ref):
    bias = bias_ref[...]
    for head in range(2):
        lanes = slice(head * HEAD_DIM, (head + 1) * HEAD_DIM)
        scaled = q_ref[:, lanes] * BF16(HEAD_DIM ** (-0.5))
        scores = dot(k_ref[:, lanes], scaled, 1, 1) + bias
        top = jnp.max(scores, axis=0, keepdims=True)
        powers = jnp.exp(scores - top)
        total = jnp.sum(powers, axis=0, keepdims=True)
        weights = (powers * (1.0 / total)).astype(BF16)
        mixed = dot(v_ref[:, lanes], weights, 0, 0)
        out_ref[:, lanes] = mixed.T.astype(BF16)
        log_ref[0, head : head + 1, :] = top + jnp.log(total)


def attention_backward(
    q_ref, k_ref, v_ref, g_ref, bias_ref, log_ref, dq_ref, dk_ref, dv_ref, dk_total, dv_total
):
    step = pl.program_id(0)

    @pl.when(step == 0)
    def _():
        dk_total[...] = jnp.zeros_like(dk_total)
        dv_total[...] = jnp.zeros_like(dv_total)

    bias = bias_ref[...]
    for head in range(2):
        lanes = slice(head * HEAD_DIM, (head + 1) * HEAD_DIM)
        scaled = q_ref[:, lanes] * BF16(HEAD_DIM ** (-0.5))
        keys, grad = k_ref[:, lanes], g_ref[:, lanes]
        scores = dot(keys, scaled, 1, 1) + bias
        probs = jnp.exp(scores - log_ref[0, head : head + 1, :])
        grad_probs = dot(v_ref[:, lanes], grad, 1, 1)
        row_dot = jnp.sum(probs * grad_probs, axis=0, keepdims=True)
        grad_scores = (probs * (grad_probs - row_dot)).astype(BF16)
        grad_q = dot(keys, grad_scores, 0, 0) * HEAD_DIM ** (-0.5)
        dq_ref[:, lanes] = grad_q.T.astype(BF16)
        dk_total[:, lanes] += dot(grad_scores, scaled, 1, 0)
        dv_total[:, lanes] += dot(probs.astype(BF16), grad, 1, 0)

    @pl.when(step == pl.num_programs(0) - 1)
    def _():
        dk_ref[...] = dk_total[...].astype(BF16)
        dv_ref[...] = dv_total[...].astype(BF16)


def attend(queries, keys, values, bias):
    rows, width = queries.shape
    block = rows // RING
    part = pl.BlockSpec((block, width), lambda i: (i, 0))
    whole = pl.BlockSpec((rows, width), lambda i: (0, 0))
    log_spec = pl.BlockSpec((1, 2, block), lambda i: (i, 0, 0))
    return pl.pallas_call(
        attention_forward,
        grid=(RING,),
        in_specs=[part, whole, whole, pl.BlockSpec((rows, 1), lambda i: (0, 0))],
        out_specs=[part, log_spec],
        out_shape=[
            jax.ShapeDtypeStruct((rows, width), BF16),
            jax.ShapeDtypeStruct((RING, 2, block), F32),
        ],
        compiler_params=pltpu.CompilerParams(vmem_limit_bytes=40 << 20),
        cost_estimate=pl.CostEstimate(
            flops=4 * rows * rows * width, bytes_accessed=8 * rows * width, transcendentals=2 * rows * rows
        ),
    )(queries, keys, values, bias)


def attend_back(queries, keys, values, grad, bias, logs):
    rows, width = queries.shape
    block = rows // RING
    part = pl.BlockSpec((block, width), lambda i: (i, 0))
    whole = pl.BlockSpec((rows, width), lambda i: (0, 0))
    log_spec = pl.BlockSpec((1, 2, block), lambda i: (i, 0, 0))
    return pl.pallas_call(
        attention_backward,
        grid=(RING,),
        in_specs=[part, whole, whole, part, pl.BlockSpec((rows, 1), lambda i: (0, 0)), log_spec],
        out_specs=[part, whole, whole],
        out_shape=[jax.ShapeDtypeStruct((rows, width), BF16)] * 3,
        scratch_shapes=[pltpu.VMEM((rows, width), F32)] * 2,
        compiler_params=pltpu.CompilerParams(vmem_limit_bytes=40 << 20),
        cost_estimate=pl.CostEstimate(
            flops=10 * rows * rows * width, bytes_accessed=14 * rows * width, transcendentals=2 * rows * rows
        ),
    )(queries, keys, values, grad, bias, logs)


def split_heads(blocks):
    return [blocks[j // 2][:, (j % 2) * 128 : (j % 2) * 128 + 128] for j in range(RING)]


def join_heads(four):
    return [jnp.concatenate([four[2 * h], four[2 * h + 1]], axis=1) for h in range(2)]


def both_slots(value, slot, core):
    half = value.shape[0] // 2
    sent = lax.dynamic_slice_in_dim(value, core * half, half, 0)
    mine = swap(sent, 2)
    other = swap(mine, 1)
    first, last = jnp.where(core == 0, mine, other), jnp.where(core == 0, other, mine)
    far = jnp.concatenate([first, last], axis=0)
    return jnp.stack([jnp.where(slot == 0, value, far), jnp.where(slot == 0, far, value)])


def per_device(
    tokens,
    cotangent,
    slot_live,
    block_rows,
    ln1_gain,
    ln1_bias,
    w_qkv,
    b_qv,
    w_proj,
    b_proj,
    scale_attn,
    ln2_gain,
    ln2_bias,
    w_up,
    b_up,
    w_down,
    b_down,
    scale_mlp,
):
    block_len = tokens.shape[1]
    at = positions()
    tp = lax.axis_index("tp")
    slot, core = tp // 2, tp % 2
    ctx = at["x"]

    orders = (("z", "y", "x"), ("x", "z", "y"), ("y", "x", "z"))
    full_qkv = [gather(w_qkv[:, c], orders[c], at) for c in range(3)]
    full_qkv, (w_up, w_down, w_proj) = lax.optimization_barrier((full_qkv, (w_up, w_down, w_proj)))
    full_proj = gather(w_proj, ("x", "z", "y"), at)
    full_up = gather(w_up, ("z", "y", "x"), at)
    full_down = gather(w_down, ("x", "y", "z"), at)
    biases = jnp.concatenate([b_qv.reshape(-1), b_up])
    other_biases = swap(biases, 2)
    biases = [jnp.where(slot == h, biases, other_biases) for h in range(2)]
    half_qv = b_qv.shape[1]

    counts = lax.dynamic_index_in_dim(block_rows, slot, 0, keepdims=False)
    live = lax.dynamic_index_in_dim(slot_live, slot, 0, keepdims=False) > 0
    within = jnp.arange(block_len, dtype=jnp.int32)
    key_valid = (within[None, :] < counts[:, None]) & live
    key_bias = jnp.where(key_valid, 0.0, MASKED).astype(F32).reshape(-1, 1)
    row_mask = (
        ((within < lax.dynamic_index_in_dim(counts, ctx, 0, keepdims=False)) & live)
        .astype(F32)[:, None]
    )

    source = lax.dynamic_index_in_dim(tokens, slot, 0, keepdims=False).astype(F32)
    normal_one, inverse_one = layer_stats(source)
    normed = (normal_one * ln1_gain + ln1_bias).astype(BF16)
    shifts = [
        [biases[h][:half_qv] for h in range(2)],
        None,
        [biases[h][half_qv : 2 * half_qv] for h in range(2)],
    ]
    mixed = []
    for c in range(3):
        columns = []
        for h in range(2):
            value = dot(normed, full_qkv[c][h], 1, 0)
            columns.append((value if shifts[c] is None else value + shifts[c][h]).astype(BF16))
        mixed.append(split_heads(columns))
    sent = jnp.stack([jnp.stack([mixed[c][j] for c in range(3)]) for j in range(RING)])
    heads = exchange(sent, ctx)
    queries, keys, values = (heads[:, c].reshape(RING * block_len, 128) for c in range(3))
    mixed_values, logs = attend(queries, keys, values, key_bias)
    attended = join_heads(exchange(mixed_values.reshape(RING, block_len, 128), ctx))
    attn_part = dot(attended[0], full_proj[0], 1, 1) + dot(attended[1], full_proj[1], 1, 1)
    branch_attn = pair_sum(attn_part) + b_proj
    middle = source + scale_attn * branch_attn

    normal_two, inverse_two = layer_stats(middle)
    second = (normal_two * ln2_gain + ln2_bias).astype(BF16)
    grad_out = row_mask * lax.dynamic_index_in_dim(cotangent, slot, 0, keepdims=False).astype(F32)
    grad_branch_mlp = (grad_out * scale_mlp).astype(BF16)
    grad_b_down = jnp.sum(grad_branch_mlp.astype(F32), axis=0)
    active, grad_hidden = [], []
    for h in range(2):
        hidden = dot(second, full_up[h], 1, 0) + biases[h][2 * half_qv :]
        below = 0.5 * (1.0 + lax.erf(hidden * 0.7071067811865476))
        slope = below + hidden * (jnp.exp(-0.5 * hidden * hidden) * 0.3989422804014327)
        active.append((hidden * below).astype(BF16))
        grad_active = dot(grad_branch_mlp, full_down[h], 1, 0)
        grad_hidden.append((grad_active * slope).astype(BF16))
    second_part = dot(grad_hidden[0], full_up[0], 1, 1) + dot(grad_hidden[1], full_up[1], 1, 1)
    grad_second = pair_sum(second_part)
    mlp_part = dot(active[0], full_down[0], 1, 1) + dot(active[1], full_down[1], 1, 1)
    branch_mlp = pair_sum(mlp_part) + b_down
    result_here = (row_mask * (middle + scale_mlp * branch_mlp)).astype(BF16)
    grad_scale_mlp = jnp.sum(grad_out * branch_mlp, axis=0)
    grad_b_up = [jnp.sum(grad_hidden[h].astype(F32), axis=0) for h in range(2)]
    grad_w_down = [dot(grad_branch_mlp, active[h], 0, 0).astype(BF16) for h in range(2)]
    grad_w_up = [dot(second, grad_hidden[h], 0, 0).astype(BF16) for h in range(2)]

    grad_ln2_gain = jnp.sum(grad_second * normal_two, axis=0)
    grad_ln2_bias = jnp.sum(grad_second, axis=0)
    grad_middle = grad_out + norm_back(grad_second * ln2_gain, normal_two, inverse_two)
    grad_scale_attn = jnp.sum(grad_middle * branch_attn, axis=0)
    grad_branch = (grad_middle * scale_attn).astype(BF16)
    grad_b_proj = jnp.sum(grad_branch.astype(F32), axis=0)
    grad_attended = [dot(grad_branch, full_proj[h], 1, 0).astype(BF16) for h in range(2)]
    grad_heads = exchange(jnp.stack(split_heads(grad_attended)), ctx).reshape(RING * block_len, 128)
    grad_w_proj = [dot(grad_branch, attended[h], 0, 0).astype(BF16) for h in range(2)]
    three = attend_back(queries, keys, values, grad_heads, key_bias, logs)
    returned = exchange(
        jnp.stack([value.reshape(RING, block_len, 128) for value in three], axis=1), ctx
    )
    grad_mixed = [join_heads(returned[:, c]) for c in range(3)]
    normed_part = sum(
        dot(grad_mixed[c][h], full_qkv[c][h], 1, 1) for c in range(3) for h in range(2)
    )
    grad_normed = pair_sum(normed_part)
    grad_ln1_gain = jnp.sum(grad_normed * normal_one, axis=0)
    grad_ln1_bias = jnp.sum(grad_normed, axis=0)
    tokens_here = grad_middle + norm_back(grad_normed * ln1_gain, normal_one, inverse_one)
    grad_w_qkv = [
        [dot(normed, grad_mixed[c][h], 0, 0).astype(BF16) for h in range(2)] for c in range(3)
    ]
    grad_b_qv = [
        jnp.sum(grad_mixed[c][h].astype(F32), axis=0) for h in range(2) for c in (0, 2)
    ]

    w_down_here = scatter_sum(grad_w_down, ("z", "y", "x"), at)
    w_up_here = scatter_sum(grad_w_up, ("x", "y", "z"), at)
    w_proj_here = scatter_sum(grad_w_proj, ("y", "z", "x"), at)
    w_qkv_here = jnp.stack(
        [scatter_sum(grad_w_qkv[c], orders[c][::-1], at) for c in range(3)], axis=1
    )
    wide = [
        grad_ln1_gain,
        grad_ln1_bias,
        grad_b_proj,
        grad_scale_attn,
        grad_ln2_gain,
        grad_ln2_bias,
        grad_b_down,
        grad_scale_mlp,
    ]
    vector = jnp.concatenate(wide + grad_b_qv + grad_b_up)
    vector = sum_everywhere(vector.reshape(-1, 128), at).reshape(-1)
    width = tokens.shape[2]
    sums = [vector[i * width : (i + 1) * width] for i in range(len(wide))]
    rest = vector[len(wide) * width :]
    qv_here = lax.dynamic_slice_in_dim(rest, slot * 2 * half_qv, 2 * half_qv, 0).reshape(2, half_qv)
    up_len = b_up.shape[0]
    up_here = lax.dynamic_slice_in_dim(rest, 4 * half_qv + slot * up_len, up_len, 0)
    result = both_slots(result_here, slot, core)
    d_tokens = both_slots(tokens_here.astype(BF16), slot, core).astype(F32)
    return (
        result,
        d_tokens,
        sums[0],
        sums[1],
        w_qkv_here,
        qv_here,
        w_proj_here,
        sums[2],
        sums[3],
        sums[4],
        sums[5],
        w_up_here,
        up_here,
        w_down_here,
        sums[6],
        sums[7],
    )


def solution(mesh):
    placed = (
        P("shard", "ctx", None),
        P("shard", "ctx", None),
        P("shard"),
        P("shard", None),
        P(),
        P(),
        P(("shard", "ctx"), None, "tp"),
        P(None, "tp"),
        P(("shard", "ctx"), "tp"),
        P(),
        P(),
        P(),
        P(),
        P(("shard", "ctx"), "tp"),
        P("tp"),
        P(("shard", "ctx"), "tp"),
        P(),
        P(),
    )
    return jax.shard_map(
        per_device,
        mesh=mesh,
        in_specs=placed,
        out_specs=(
            P("shard", "ctx", None),
            P("shard", "ctx", None),
            P(),
            P(),
            P(("shard", "ctx"), None, "tp"),
            P(None, "tp"),
            P(("shard", "ctx"), "tp"),
            P(),
            P(),
            P(),
            P(),
            P(("shard", "ctx"), "tp"),
            P("tp"),
            P(("shard", "ctx"), "tp"),
            P(),
            P(),
        ),
        check_vma=False,
    )
```

```python
import jax
import jax.numpy as jnp
from jax import lax
from jax.experimental import pallas as pl
from jax.experimental.pallas import tpu as pltpu
from jax.sharding import PartitionSpec as P

HEAD_DIM = 64
EPSILON = 1e-06
MASKED = -1e30
RING = 4
BF16 = jnp.bfloat16
F32 = jnp.float32

AXES = (("y_lo", 2), ("z", RING), ("x", RING), ("y_hi", 2), ("core", 2))
DIM = {"y": 0, "z": 1, "x": 2}
ORDERS = (("z", "y", "x"), ("x", "z", "y"), ("y", "x", "z"))


def step_ring(value, axis, step):
    names = ("y_lo", "y_hi", "core") if axis == "y" else (axis, "core")
    place = (lambda p: (p % 2) * 2 + p // 2) if axis == "y" else (lambda p: p)
    pairs = [
        (place(p) * 2 + core, place((p + (-step if core else step)) % RING) * 2 + core)
        for p in range(RING)
        for core in range(2)
    ]
    return lax.ppermute(value, names, pairs)


def swap(value, axis, bit=1):
    return lax.ppermute(value, axis, [(i, i ^ bit) for i in range(lax.axis_size(axis))])


def positions():
    return {
        "x": lax.axis_index("x"),
        "z": lax.axis_index("z"),
        "y": 2 * lax.axis_index("y_hi") + lax.axis_index("y_lo"),
    }


def gather_axis(value, axis, at, way):
    dim = DIM[axis]
    size = value.shape[dim]
    behind = step_ring(value, axis, 1)
    two = step_ring(jnp.concatenate([value, behind], dim), axis, 2)
    parts = [value, behind] + [lax.slice_in_dim(two, i * size, (i + 1) * size, axis=dim) for i in (0, 1)]
    shape = list(value.shape)
    shape[dim] *= RING
    out = jnp.zeros(shape, value.dtype)
    for step, part in enumerate(parts):
        out = lax.dynamic_update_slice_in_dim(out, part, ((at[axis] - step * way) % RING) * size, dim)
    return out


def gather(chunk, order, at, way):
    value = chunk[None, None, None]
    for axis in order:
        value = gather_axis(value, axis, at, way)
    return value.reshape(2, RING * RING * 2 * chunk.shape[0], chunk.shape[1])


def scatter_axis(value, axis, at, way):
    dim = DIM[axis]

    def block(step):
        return lax.dynamic_slice_in_dim(value, (at[axis] + step * way) % RING, 1, dim)

    far = step_ring(jnp.concatenate([block(2), block(3)], dim), axis, 2)
    here, next_one = (lax.slice_in_dim(far, i, i + 1, axis=dim).astype(F32) for i in (0, 1))
    near = step_ring((block(1).astype(F32) + next_one).astype(BF16), axis, 1)
    return block(0).astype(F32) + here + near.astype(F32)


def scatter_sum(halves, order, at, way):
    rows, columns = halves[0].shape
    value = jnp.stack(halves).reshape(RING, RING, RING, rows // 32, columns)
    for place, axis in enumerate(order):
        total = scatter_axis(value, axis, at, way)
        value = total if place == len(order) - 1 else total.astype(BF16)
    return value.reshape(rows // 32, columns)


def sum_everywhere(vector):
    for axis, bit in (("x", 1), ("x", 2), ("z", 1), ("z", 2), ("y_lo", 1), ("y_hi", 1)):
        vector = vector + swap(vector, axis, bit)
    return vector


def exchange(blocks):
    return lax.all_to_all(blocks, "x", split_axis=0, concat_axis=0, tiled=True)


def layer_stats(values):
    average = jnp.mean(values, axis=-1, keepdims=True)
    centered = values - average
    variance = jnp.mean(centered * centered, axis=-1, keepdims=True)
    inverse = lax.rsqrt(variance + EPSILON)
    return (centered * inverse, inverse)


def norm_back(grad_hat, normal_hat, inverse):
    first_term = jnp.mean(grad_hat, axis=-1, keepdims=True)
    second_term = jnp.mean(grad_hat * normal_hat, axis=-1, keepdims=True)
    return inverse * (grad_hat - first_term - normal_hat * second_term)


def dot(left, right, left_dim, right_dim):
    return lax.dot_general(
        left, right, (((left_dim,), (right_dim,)), ((), ())), preferred_element_type=F32
    )


def pair_sum(part):
    low = part.astype(BF16)
    return low.astype(F32) + swap(low, "core").astype(F32)


def attention_forward(q_ref, k_ref, v_ref, bias_ref, out_ref, log_ref):
    bias = bias_ref[...]
    for head in range(2):
        lanes = slice(head * HEAD_DIM, (head + 1) * HEAD_DIM)
        scaled = q_ref[:, lanes] * BF16(HEAD_DIM ** (-0.5))
        scores = dot(k_ref[:, lanes], scaled, 1, 1) + bias
        top = jnp.max(scores, axis=0, keepdims=True)
        powers = jnp.exp(scores - top)
        total = jnp.sum(powers, axis=0, keepdims=True)
        weights = (powers * (1.0 / total)).astype(BF16)
        mixed = dot(v_ref[:, lanes], weights, 0, 0)
        out_ref[:, lanes] = mixed.T.astype(BF16)
        log_ref[0, head : head + 1, :] = top + jnp.log(total)


def attention_backward(
    q_ref, k_ref, v_ref, g_ref, bias_ref, log_ref, dq_ref, dk_ref, dv_ref, dk_total, dv_total
):
    step = pl.program_id(0)

    @pl.when(step == 0)
    def _():
        dk_total[...] = jnp.zeros_like(dk_total)
        dv_total[...] = jnp.zeros_like(dv_total)

    bias = bias_ref[...]
    for head in range(2):
        lanes = slice(head * HEAD_DIM, (head + 1) * HEAD_DIM)
        scaled = q_ref[:, lanes] * BF16(HEAD_DIM ** (-0.5))
        keys, grad = k_ref[:, lanes], g_ref[:, lanes]
        scores = dot(keys, scaled, 1, 1) + bias
        probs = jnp.exp(scores - log_ref[0, head : head + 1, :])
        grad_probs = dot(v_ref[:, lanes], grad, 1, 1)
        row_dot = jnp.sum(probs * grad_probs, axis=0, keepdims=True)
        grad_scores = (probs * (grad_probs - row_dot)).astype(BF16)
        grad_q = dot(keys, grad_scores, 0, 0) * HEAD_DIM ** (-0.5)
        dq_ref[:, lanes] = grad_q.T.astype(BF16)
        dk_total[:, lanes] += dot(grad_scores, scaled, 1, 0)
        dv_total[:, lanes] += dot(probs.astype(BF16), grad, 1, 0)

    @pl.when(step == pl.num_programs(0) - 1)
    def _():
        dk_ref[...] = dk_total[...].astype(BF16)
        dv_ref[...] = dv_total[...].astype(BF16)


def attend(queries, keys, values, bias):
    rows, width = queries.shape
    block = rows // RING
    part = pl.BlockSpec((block, width), lambda i: (i, 0))
    whole = pl.BlockSpec((rows, width), lambda i: (0, 0))
    log_spec = pl.BlockSpec((1, 2, block), lambda i: (i, 0, 0))
    return pl.pallas_call(
        attention_forward,
        grid=(RING,),
        in_specs=[part, whole, whole, pl.BlockSpec((rows, 1), lambda i: (0, 0))],
        out_specs=[part, log_spec],
        out_shape=[
            jax.ShapeDtypeStruct((rows, width), BF16),
            jax.ShapeDtypeStruct((RING, 2, block), F32),
        ],
        compiler_params=pltpu.CompilerParams(vmem_limit_bytes=40 << 20),
        cost_estimate=pl.CostEstimate(
            flops=4 * rows * rows * width, bytes_accessed=8 * rows * width, transcendentals=2 * rows * rows
        ),
    )(queries, keys, values, bias)


def attend_back(queries, keys, values, grad, bias, logs):
    rows, width = queries.shape
    block = rows // RING
    part = pl.BlockSpec((block, width), lambda i: (i, 0))
    whole = pl.BlockSpec((rows, width), lambda i: (0, 0))
    log_spec = pl.BlockSpec((1, 2, block), lambda i: (i, 0, 0))
    return pl.pallas_call(
        attention_backward,
        grid=(RING,),
        in_specs=[part, whole, whole, part, pl.BlockSpec((rows, 1), lambda i: (0, 0)), log_spec],
        out_specs=[part, whole, whole],
        out_shape=[jax.ShapeDtypeStruct((rows, width), BF16)] * 3,
        scratch_shapes=[pltpu.VMEM((rows, width), F32)] * 2,
        compiler_params=pltpu.CompilerParams(vmem_limit_bytes=40 << 20),
        cost_estimate=pl.CostEstimate(
            flops=10 * rows * rows * width, bytes_accessed=14 * rows * width, transcendentals=2 * rows * rows
        ),
    )(queries, keys, values, grad, bias, logs)


def split_heads(blocks):
    return [blocks[j // 2][:, (j % 2) * 128 : (j % 2) * 128 + 128] for j in range(RING)]


def join_heads(four):
    return [jnp.concatenate([four[2 * h], four[2 * h + 1]], axis=1) for h in range(2)]


def both_slots(value, slot, core):
    half = value.shape[0] // 2
    sent = lax.dynamic_slice_in_dim(value, core * half, half, 0)
    mine = swap(sent, "y_hi")
    other = swap(mine, "core")
    first, last = jnp.where(core == 0, mine, other), jnp.where(core == 0, other, mine)
    far = jnp.concatenate([first, last], axis=0)
    return jnp.stack([jnp.where(slot == 0, value, far), jnp.where(slot == 0, far, value)])


def per_device(
    tokens,
    cotangent,
    slot_live,
    block_rows,
    ln1_gain,
    ln1_bias,
    w_qkv,
    b_qv,
    w_proj,
    b_proj,
    scale_attn,
    ln2_gain,
    ln2_bias,
    w_up,
    b_up,
    w_down,
    b_down,
    scale_mlp,
):
    block_len = tokens.shape[1]
    at = positions()
    slot, core = lax.axis_index("y_hi"), lax.axis_index("core")
    ctx = at["x"]
    way = 1 - 2 * core

    cuts = (w_up.shape[1], w_up.shape[1] + w_down.shape[1])
    others = lax.all_gather(
        jnp.concatenate([w_up, w_down, w_proj], axis=1), ("y_hi", "y_lo", "z", "x"), axis=0, tiled=True
    )
    others = others.reshape(2, -1, others.shape[1])
    full_up = [others[h, :, : cuts[0]] for h in range(2)]
    full_down = [others[h, :, cuts[0] : cuts[1]] for h in range(2)]
    full_proj = [others[h, :, cuts[1] :] for h in range(2)]
    full_qkv = [gather(w_qkv[:, c], ORDERS[c], at, way) for c in range(3)]
    biases = jnp.concatenate([b_qv.reshape(-1), b_up])
    other_biases = swap(biases, "y_hi")
    biases = [jnp.where(slot == h, biases, other_biases) for h in range(2)]
    half_qv = b_qv.shape[1]

    counts = lax.dynamic_index_in_dim(block_rows, slot, 0, keepdims=False)
    live = lax.dynamic_index_in_dim(slot_live, slot, 0, keepdims=False) > 0
    within = jnp.arange(block_len, dtype=jnp.int32)
    key_valid = (within[None, :] < counts[:, None]) & live
    key_bias = jnp.where(key_valid, 0.0, MASKED).astype(F32).reshape(-1, 1)
    row_mask = (
        ((within < lax.dynamic_index_in_dim(counts, ctx, 0, keepdims=False)) & live)
        .astype(F32)[:, None]
    )

    source = lax.dynamic_index_in_dim(tokens, slot, 0, keepdims=False).astype(F32)
    normal_one, inverse_one = layer_stats(source)
    normed = (normal_one * ln1_gain + ln1_bias).astype(BF16)
    shifts = [
        [biases[h][:half_qv] for h in range(2)],
        None,
        [biases[h][half_qv : 2 * half_qv] for h in range(2)],
    ]
    mixed = []
    for c in range(3):
        columns = []
        for h in range(2):
            value = dot(normed, full_qkv[c][h], 1, 0)
            columns.append((value if shifts[c] is None else value + shifts[c][h]).astype(BF16))
        mixed.append(split_heads(columns))
    sent = jnp.stack([jnp.stack([mixed[c][j] for c in range(3)]) for j in range(RING)])
    heads = exchange(sent)
    queries, keys, values = (heads[:, c].reshape(RING * block_len, 128) for c in range(3))
    mixed_values, logs = attend(queries, keys, values, key_bias)
    attended = join_heads(exchange(mixed_values.reshape(RING, block_len, 128)))
    attn_part = dot(attended[0], full_proj[0], 1, 1) + dot(attended[1], full_proj[1], 1, 1)
    branch_attn = pair_sum(attn_part) + b_proj
    middle = source + scale_attn * branch_attn

    normal_two, inverse_two = layer_stats(middle)
    second = (normal_two * ln2_gain + ln2_bias).astype(BF16)
    grad_out = row_mask * lax.dynamic_index_in_dim(cotangent, slot, 0, keepdims=False).astype(F32)
    grad_branch_mlp = (grad_out * scale_mlp).astype(BF16)
    grad_b_down = jnp.sum(grad_branch_mlp.astype(F32), axis=0)
    active, grad_hidden = [], []
    for h in range(2):
        hidden = dot(second, full_up[h], 1, 0) + biases[h][2 * half_qv :]
        below = 0.5 * (1.0 + lax.erf(hidden * 0.7071067811865476))
        slope = below + hidden * (jnp.exp(-0.5 * hidden * hidden) * 0.3989422804014327)
        active.append((hidden * below).astype(BF16))
        grad_active = dot(grad_branch_mlp, full_down[h], 1, 0)
        grad_hidden.append((grad_active * slope).astype(BF16))
    second_part = dot(grad_hidden[0], full_up[0], 1, 1) + dot(grad_hidden[1], full_up[1], 1, 1)
    grad_second = pair_sum(second_part)
    mlp_part = dot(active[0], full_down[0], 1, 1) + dot(active[1], full_down[1], 1, 1)
    branch_mlp = pair_sum(mlp_part) + b_down
    result_here = (row_mask * (middle + scale_mlp * branch_mlp)).astype(BF16)
    grad_scale_mlp = jnp.sum(grad_out * branch_mlp, axis=0)
    grad_b_up = [jnp.sum(grad_hidden[h].astype(F32), axis=0) for h in range(2)]
    grad_w_down = [dot(grad_branch_mlp, active[h], 0, 0).astype(BF16) for h in range(2)]
    grad_w_up = [dot(second, grad_hidden[h], 0, 0).astype(BF16) for h in range(2)]

    grad_ln2_gain = jnp.sum(grad_second * normal_two, axis=0)
    grad_ln2_bias = jnp.sum(grad_second, axis=0)
    grad_middle = grad_out + norm_back(grad_second * ln2_gain, normal_two, inverse_two)
    grad_scale_attn = jnp.sum(grad_middle * branch_attn, axis=0)
    grad_branch = (grad_middle * scale_attn).astype(BF16)
    grad_b_proj = jnp.sum(grad_branch.astype(F32), axis=0)
    grad_attended = [dot(grad_branch, full_proj[h], 1, 0).astype(BF16) for h in range(2)]
    grad_heads = exchange(jnp.stack(split_heads(grad_attended))).reshape(RING * block_len, 128)
    grad_w_proj = [dot(grad_branch, attended[h], 0, 0).astype(BF16) for h in range(2)]
    three = attend_back(queries, keys, values, grad_heads, key_bias, logs)
    returned = exchange(
        jnp.stack([value.reshape(RING, block_len, 128) for value in three], axis=1)
    )
    grad_mixed = [join_heads(returned[:, c]) for c in range(3)]
    normed_part = sum(
        dot(grad_mixed[c][h], full_qkv[c][h], 1, 1) for c in range(3) for h in range(2)
    )
    grad_normed = pair_sum(normed_part)
    grad_ln1_gain = jnp.sum(grad_normed * normal_one, axis=0)
    grad_ln1_bias = jnp.sum(grad_normed, axis=0)
    tokens_here = grad_middle + norm_back(grad_normed * ln1_gain, normal_one, inverse_one)
    grad_w_qkv = [
        [dot(normed, grad_mixed[c][h], 0, 0).astype(BF16) for h in range(2)] for c in range(3)
    ]
    grad_b_qv = [
        jnp.sum(grad_mixed[c][h].astype(F32), axis=0) for h in range(2) for c in (0, 2)
    ]

    joined = jnp.concatenate(
        [jnp.stack(halves) for halves in (grad_w_up, grad_w_down, grad_w_proj)], axis=2
    )
    width, chunk = joined.shape[2], w_up.shape[0]
    joined = joined.reshape(RING, RING * RING, chunk, width).swapaxes(0, 1).reshape(-1, width)
    joined = lax.psum_scatter(joined, ("z", "x"), scatter_dimension=0, tiled=True)
    joined = scatter_axis(joined.reshape(RING, 1, 1, chunk, width), "y", at, way).reshape(chunk, width)
    w_up_here, w_down_here, w_proj_here = jnp.split(joined, cuts, axis=1)
    w_qkv_here = jnp.stack(
        [scatter_sum(grad_w_qkv[c], ORDERS[c][::-1], at, way) for c in range(3)], axis=1
    )
    wide = [
        grad_ln1_gain,
        grad_ln1_bias,
        grad_b_proj,
        grad_scale_attn,
        grad_ln2_gain,
        grad_ln2_bias,
        grad_b_down,
        grad_scale_mlp,
    ]
    vector = jnp.concatenate(wide + grad_b_qv + grad_b_up)
    vector = sum_everywhere(vector.reshape(-1, 128)).reshape(-1)
    width = tokens.shape[2]
    sums = [vector[i * width : (i + 1) * width] for i in range(len(wide))]
    rest = vector[len(wide) * width :]
    qv_here = lax.dynamic_slice_in_dim(rest, slot * 2 * half_qv, 2 * half_qv, 0).reshape(2, half_qv)
    up_len = b_up.shape[0]
    up_here = lax.dynamic_slice_in_dim(rest, 4 * half_qv + slot * up_len, up_len, 0)
    result = both_slots(result_here, slot, core)
    d_tokens = both_slots(tokens_here.astype(BF16), slot, core).astype(F32)
    return (
        result,
        d_tokens,
        sums[0],
        sums[1],
        w_qkv_here,
        qv_here,
        w_proj_here,
        sums[2],
        sums[3],
        sums[4],
        sums[5],
        w_up_here,
        up_here,
        w_down_here,
        sums[6],
        sums[7],
    )


def solution(mesh):
    torus = jax.sharding.Mesh(
        mesh.devices.reshape([size for _, size in AXES]), [name for name, _ in AXES]
    )
    shard, rows, pair = ("y_lo", "z"), ("y_lo", "z", "x"), ("y_hi", "core")
    matrix = P(rows, pair)
    images = P(shard, "x", None)
    w_qkv = P(rows, None, pair)
    return jax.shard_map(
        per_device,
        mesh=torus,
        in_specs=(
            images,
            images,
            P(shard),
            P(shard, None),
            P(),
            P(),
            w_qkv,
            P(None, pair),
            matrix,
            P(),
            P(),
            P(),
            P(),
            matrix,
            P(pair),
            matrix,
            P(),
            P(),
        ),
        out_specs=(
            images,
            images,
            P(),
            P(),
            w_qkv,
            P(None, pair),
            matrix,
            P(),
            P(),
            P(),
            P(),
            matrix,
            P(pair),
            matrix,
            P(),
            P(),
        ),
        check_vma=False,
    )
```

```python
import jax
import jax.numpy as jnp
from jax import lax
from jax.experimental import pallas as pl
from jax.experimental.pallas import tpu as pltpu
from jax.sharding import PartitionSpec as P

HEAD_DIM = 64
EPSILON = 1e-06
MASKED = -1e30
RING = 4
BF16 = jnp.bfloat16
F32 = jnp.float32

AXES = (("y_lo", 2), ("z", RING), ("x", RING), ("y_hi", 2), ("core", 2))
DIM = {"y": 0, "z": 1, "x": 2}
ORDERS = (("z", "y", "x"), ("x", "z", "y"), ("y", "x", "z"))


def step_ring(value, axis, step):
    names = ("y_lo", "y_hi", "core") if axis == "y" else (axis, "core")
    place = (lambda p: (p % 2) * 2 + p // 2) if axis == "y" else (lambda p: p)
    pairs = [
        (place(p) * 2 + core, place((p + (-step if core else step)) % RING) * 2 + core)
        for p in range(RING)
        for core in range(2)
    ]
    return lax.ppermute(value, names, pairs)


def swap(value, axis, bit=1):
    return lax.ppermute(value, axis, [(i, i ^ bit) for i in range(lax.axis_size(axis))])


def positions():
    return {
        "x": lax.axis_index("x"),
        "z": lax.axis_index("z"),
        "y": 2 * lax.axis_index("y_hi") + lax.axis_index("y_lo"),
    }


def gather_axis(value, axis, at, way):
    dim = DIM[axis]
    size = value.shape[dim]
    behind = step_ring(value, axis, 1)
    two = step_ring(jnp.concatenate([value, behind], dim), axis, 2)
    parts = [value, behind] + [lax.slice_in_dim(two, i * size, (i + 1) * size, axis=dim) for i in (0, 1)]
    shape = list(value.shape)
    shape[dim] *= RING
    out = jnp.zeros(shape, value.dtype)
    for step, part in enumerate(parts):
        out = lax.dynamic_update_slice_in_dim(out, part, ((at[axis] - step * way) % RING) * size, dim)
    return out


def gather(chunk, order, at, way):
    value = chunk[None, None, None]
    for axis in order:
        value = gather_axis(value, axis, at, way)
    return value.reshape(2, RING * RING * 2 * chunk.shape[0], chunk.shape[1])


def scatter_axis(value, axis, at, way):
    dim = DIM[axis]

    def block(step):
        return lax.dynamic_slice_in_dim(value, (at[axis] + step * way) % RING, 1, dim)

    far = step_ring(jnp.concatenate([block(2), block(3)], dim), axis, 2)
    here, next_one = (lax.slice_in_dim(far, i, i + 1, axis=dim).astype(F32) for i in (0, 1))
    near = step_ring((block(1).astype(F32) + next_one).astype(BF16), axis, 1)
    return block(0).astype(F32) + here + near.astype(F32)


def sum_everywhere(vector):
    for axis, bit in (("x", 1), ("x", 2), ("z", 1), ("z", 2), ("y_lo", 1), ("y_hi", 1)):
        vector = vector + swap(vector, axis, bit)
    return vector


def exchange(blocks):
    return lax.all_to_all(blocks, "x", split_axis=0, concat_axis=0, tiled=True)


def layer_stats(values):
    average = jnp.mean(values, axis=-1, keepdims=True)
    centered = values - average
    variance = jnp.mean(centered * centered, axis=-1, keepdims=True)
    inverse = lax.rsqrt(variance + EPSILON)
    return (centered * inverse, inverse)


def norm_back(grad_hat, normal_hat, inverse):
    first_term = jnp.mean(grad_hat, axis=-1, keepdims=True)
    second_term = jnp.mean(grad_hat * normal_hat, axis=-1, keepdims=True)
    return inverse * (grad_hat - first_term - normal_hat * second_term)


def dot(left, right, left_dim, right_dim):
    return lax.dot_general(
        left, right, (((left_dim,), (right_dim,)), ((), ())), preferred_element_type=F32
    )


def pair_sum(part):
    low = part.astype(BF16)
    return low.astype(F32) + swap(low, "core").astype(F32)


def head_lanes(head, width):
    lanes = lax.broadcasted_iota(jnp.int32, (1, width), 1) // HEAD_DIM
    return jnp.where(lanes == head, 1.0, 0.0).astype(F32)


def attention_forward(q_ref, k_ref, v_ref, bias_ref, out_ref, log_ref, out_total):
    out_total[...] = jnp.zeros_like(out_total)

    @pl.loop(0, 2)
    def _(head):
        here = head_lanes(head, q_ref.shape[1])
        scaled = q_ref[...] * (here * HEAD_DIM ** (-0.5)).astype(BF16)
        scores = dot(k_ref[...], scaled, 1, 1) + bias_ref[...]
        top = jnp.max(scores, axis=0, keepdims=True)
        powers = jnp.exp(scores - top)
        total = jnp.sum(powers, axis=0, keepdims=True)
        weights = (powers * (1.0 / total)).astype(BF16)
        mixed = dot(v_ref[...], weights, 0, 0)
        out_total[...] += mixed.T * here
        log_ref[0, pl.ds(head, 1), :] = top + jnp.log(total)

    out_ref[...] = out_total[...].astype(BF16)


def attention_backward(
    q_ref, k_ref, v_ref, g_ref, bias_ref, log_ref, dq_ref, dk_ref, dv_ref, dq_total, dk_total, dv_total
):
    step = pl.program_id(0)

    @pl.when(step == 0)
    def _():
        dk_total[...] = jnp.zeros_like(dk_total)
        dv_total[...] = jnp.zeros_like(dv_total)

    dq_total[...] = jnp.zeros_like(dq_total)

    @pl.loop(0, 2)
    def _(head):
        here = head_lanes(head, q_ref.shape[1])
        scaled = q_ref[...] * (here * HEAD_DIM ** (-0.5)).astype(BF16)
        grad = g_ref[...] * here.astype(BF16)
        scores = dot(k_ref[...], scaled, 1, 1) + bias_ref[...]
        probs = jnp.exp(scores - log_ref[0, pl.ds(head, 1), :])
        grad_probs = dot(v_ref[...], grad, 1, 1)
        row_dot = jnp.sum(probs * grad_probs, axis=0, keepdims=True)
        grad_scores = (probs * (grad_probs - row_dot)).astype(BF16)
        dq_total[...] += dot(k_ref[...], grad_scores, 0, 0).T * (here * HEAD_DIM ** (-0.5))
        dk_total[...] += dot(grad_scores, scaled, 1, 0)
        dv_total[...] += dot(probs.astype(BF16), grad, 1, 0)

    dq_ref[...] = dq_total[...].astype(BF16)

    @pl.when(step == pl.num_programs(0) - 1)
    def _():
        dk_ref[...] = dk_total[...].astype(BF16)
        dv_ref[...] = dv_total[...].astype(BF16)


def attend(queries, keys, values, bias):
    rows, width = queries.shape
    block = rows // RING
    part = pl.BlockSpec((block, width), lambda i: (i, 0))
    whole = pl.BlockSpec((rows, width), lambda i: (0, 0))
    log_spec = pl.BlockSpec((1, 2, block), lambda i: (i, 0, 0))
    return pl.pallas_call(
        attention_forward,
        grid=(RING,),
        in_specs=[part, whole, whole, pl.BlockSpec((rows, 1), lambda i: (0, 0))],
        out_specs=[part, log_spec],
        out_shape=[
            jax.ShapeDtypeStruct((rows, width), BF16),
            jax.ShapeDtypeStruct((RING, 2, block), F32),
        ],
        scratch_shapes=[pltpu.VMEM((block, width), F32)],
        compiler_params=pltpu.CompilerParams(vmem_limit_bytes=40 << 20),
        cost_estimate=pl.CostEstimate(
            flops=4 * rows * rows * width, bytes_accessed=8 * rows * width, transcendentals=2 * rows * rows
        ),
    )(queries, keys, values, bias)


def attend_back(queries, keys, values, grad, bias, logs):
    rows, width = queries.shape
    block = rows // RING
    part = pl.BlockSpec((block, width), lambda i: (i, 0))
    whole = pl.BlockSpec((rows, width), lambda i: (0, 0))
    log_spec = pl.BlockSpec((1, 2, block), lambda i: (i, 0, 0))
    return pl.pallas_call(
        attention_backward,
        grid=(RING,),
        in_specs=[part, whole, whole, part, pl.BlockSpec((rows, 1), lambda i: (0, 0)), log_spec],
        out_specs=[part, whole, whole],
        out_shape=[jax.ShapeDtypeStruct((rows, width), BF16)] * 3,
        scratch_shapes=[pltpu.VMEM((block, width), F32)] + [pltpu.VMEM((rows, width), F32)] * 2,
        compiler_params=pltpu.CompilerParams(vmem_limit_bytes=40 << 20),
        cost_estimate=pl.CostEstimate(
            flops=10 * rows * rows * width, bytes_accessed=14 * rows * width, transcendentals=2 * rows * rows
        ),
    )(queries, keys, values, grad, bias, logs)


def feed_forward(
    x_ref, g_ref, up_ref, down_ref, bias_ref, act_ref, hid_ref, out_ref, back_ref, sum_ref, out_total, back_total
):
    step = pl.program_id(0)

    @pl.when(step == 0)
    def _():
        out_total[...] = jnp.zeros_like(out_total)
        back_total[...] = jnp.zeros_like(back_total)

    up, down = up_ref[0], down_ref[0]
    hidden = dot(x_ref[...], up, 1, 0) + bias_ref[0]
    below = 0.5 * (1.0 + lax.erf(hidden * 0.7071067811865476))
    slope = below + hidden * (jnp.exp(-0.5 * hidden * hidden) * 0.3989422804014327)
    active = (hidden * below).astype(BF16)
    grad_hidden = (dot(g_ref[...], down, 1, 0) * slope).astype(BF16)
    act_ref[...] = active
    hid_ref[...] = grad_hidden
    sum_ref[0] = jnp.sum(grad_hidden.astype(F32), axis=0, keepdims=True)
    out_total[...] += dot(active, down, 1, 1)
    back_total[...] += dot(grad_hidden, up, 1, 1)

    @pl.when(step == pl.num_programs(0) - 1)
    def _():
        out_ref[...] = out_total[...].astype(BF16)
        back_ref[...] = back_total[...].astype(BF16)


def feed_forward_both_ways(second, grad, weights, bias):
    rows, width = second.shape
    steps = bias.shape[0]
    half = steps // 2
    whole = pl.BlockSpec((rows, width), lambda j: (0, 0))
    part = pl.BlockSpec((rows, 256), lambda j: (0, j))
    small = pl.BlockSpec((1, 1, 256), lambda j: (j, 0, 0))
    return pl.pallas_call(
        feed_forward,
        grid=(steps,),
        in_specs=[
            whole,
            whole,
            pl.BlockSpec((1, width, 256), lambda j: (j // half, 0, j % half)),
            pl.BlockSpec((1, width, 256), lambda j: (j // half, 0, half + j % half)),
            small,
        ],
        out_specs=[part, part, whole, whole, small],
        out_shape=[jax.ShapeDtypeStruct((rows, 256 * steps), BF16)] * 2
        + [jax.ShapeDtypeStruct((rows, width), BF16)] * 2
        + [jax.ShapeDtypeStruct((steps, 1, 256), F32)],
        scratch_shapes=[pltpu.VMEM((rows, width), F32)] * 2,
        compiler_params=pltpu.CompilerParams(vmem_limit_bytes=40 << 20),
        cost_estimate=pl.CostEstimate(
            flops=8 * rows * width * 256 * steps,
            bytes_accessed=4 * width * 256 * steps,
            transcendentals=2 * rows * 256 * steps,
        ),
    )(second, grad, weights, weights, bias)


def joined_gradient(second_ref, mlp_ref, attn_ref, hid_ref, act_ref, att_ref, out_ref):
    block = pl.program_id(0) % 9

    def write(left_ref, right_ref):
        value = dot(left_ref[...], right_ref[...], 1, 0).astype(BF16)
        chunk = value.shape[0] // (2 * RING * RING)
        for y_lo in range(2):
            for place in range(RING * RING):
                rows = value[(y_lo * RING * RING + place) * chunk :][:chunk]
                out_ref[pl.ds((place * 2 + y_lo) * chunk, chunk), :] = rows

    @pl.when(block < 4)
    def _():
        write(second_ref, hid_ref)

    @pl.when((block >= 4) & (block < 8))
    def _():
        write(mlp_ref, act_ref)

    @pl.when(block == 8)
    def _():
        write(attn_ref, att_ref)


def gradient_cost(rows, depth, columns):
    return pl.CostEstimate(
        flops=2 * rows * depth * columns, bytes_accessed=2 * rows * columns, transcendentals=0
    )


def joined_gradients(lefts, rights):
    rows, depth = lefts[0].shape
    columns = sum(right.shape[1] for right in rights)
    whole = pl.BlockSpec((rows, depth), lambda j: (0, 0))
    return pl.pallas_call(
        joined_gradient,
        grid=(columns // 256,),
        in_specs=[
            whole,
            whole,
            whole,
            pl.BlockSpec((depth, 256), lambda j: (0, j // 9 * 4 + jnp.minimum(j % 9, 3))),
            pl.BlockSpec((depth, 256), lambda j: (0, j // 9 * 4 + jnp.clip(j % 9 - 4, 0, 3))),
            pl.BlockSpec((depth, 256), lambda j: (0, j // 9)),
        ],
        out_specs=pl.BlockSpec((rows, 256), lambda j: (0, j)),
        out_shape=jax.ShapeDtypeStruct((rows, columns), BF16),
        compiler_params=pltpu.CompilerParams(vmem_limit_bytes=40 << 20),
        cost_estimate=gradient_cost(rows, depth, columns),
    )(*lefts, *rights)


def qkv_gradient(left_ref, grad_ref, q_ref, k_ref, v_ref, out_ref, back_ref, sum_ref, back_total):
    step = pl.program_id(0)

    @pl.when(step == 0)
    def _():
        back_total[...] = jnp.zeros_like(back_total)

    for c, weights in enumerate((q_ref, k_ref, v_ref)):
        grad = grad_ref[0, c]
        value = dot(left_ref[...], grad, 1, 0).astype(BF16)
        out_ref[0, :, c] = value.reshape(out_ref.shape[1], out_ref.shape[3], out_ref.shape[4])
        back_total[...] += dot(grad, weights[0], 1, 1)
        sum_ref[0, c : c + 1, :] = jnp.sum(grad.astype(F32), axis=0, keepdims=True)

    @pl.when(step == pl.num_programs(0) - 1)
    def _():
        back_ref[...] = back_total[...].astype(BF16)


def qkv_gradients(left, grads, weights, chunk):
    width, rows = left.shape
    weight = pl.BlockSpec((1, width, 128), lambda j: (j // 2, 0, j % 2))
    return pl.pallas_call(
        qkv_gradient,
        grid=(RING,),
        in_specs=[
            pl.BlockSpec((width, rows), lambda j: (0, 0)),
            pl.BlockSpec((1, 3, rows, 128), lambda j: (j, 0, 0, 0)),
            weight,
            weight,
            weight,
        ],
        out_specs=[
            pl.BlockSpec((1, width // chunk, 3, chunk, 128), lambda j: (j // 2, 0, 0, 0, j % 2)),
            pl.BlockSpec((rows, width), lambda j: (0, 0)),
            pl.BlockSpec((1, 3, 128), lambda j: (j, 0, 0)),
        ],
        out_shape=[
            jax.ShapeDtypeStruct((2, width // chunk, 3, chunk, 256), BF16),
            jax.ShapeDtypeStruct((rows, width), BF16),
            jax.ShapeDtypeStruct((RING, 3, 128), F32),
        ],
        scratch_shapes=[pltpu.VMEM((rows, width), F32)],
        compiler_params=pltpu.CompilerParams(vmem_limit_bytes=40 << 20),
        cost_estimate=gradient_cost(2 * width, rows, 12 * 128),
    )(left, grads, *weights)


def split_heads(blocks):
    return [blocks[j // 2][:, (j % 2) * 128 : (j % 2) * 128 + 128] for j in range(RING)]


def join_heads(four):
    return [jnp.concatenate([four[2 * h], four[2 * h + 1]], axis=1) for h in range(2)]


def both_slots(value, slot, core):
    half = value.shape[0] // 2
    sent = lax.dynamic_slice_in_dim(value, core * half, half, 0)
    mine = swap(sent, "y_hi")
    other = swap(mine, "core")
    first, last = jnp.where(core == 0, mine, other), jnp.where(core == 0, other, mine)
    far = jnp.concatenate([first, last], axis=0)
    return jnp.stack([jnp.where(slot == 0, value, far), jnp.where(slot == 0, far, value)])


def per_device(
    tokens,
    cotangent,
    slot_live,
    block_rows,
    ln1_gain,
    ln1_bias,
    w_qkv,
    b_qv,
    w_proj,
    b_proj,
    scale_attn,
    ln2_gain,
    ln2_bias,
    w_up,
    b_up,
    w_down,
    b_down,
    scale_mlp,
):
    block_len = tokens.shape[1]
    at = positions()
    slot, core = lax.axis_index("y_hi"), lax.axis_index("core")
    ctx = at["x"]
    way = 1 - 2 * core

    cuts = (w_up.shape[1], w_up.shape[1] + w_down.shape[1])
    others = lax.all_gather(
        jnp.concatenate([w_up, w_down, w_proj], axis=1), ("y_hi", "y_lo", "z", "x"), axis=0, tiled=True
    )
    others = others.reshape(2, -1, others.shape[1])
    full_proj = [others[h, :, cuts[1] :] for h in range(2)]
    full_qkv = [gather(w_qkv[:, c], ORDERS[c], at, way) for c in range(3)]
    biases = jnp.concatenate([b_qv.reshape(-1), b_up])
    other_biases = swap(biases, "y_hi")
    biases = [jnp.where(slot == h, biases, other_biases) for h in range(2)]
    half_qv = b_qv.shape[1]

    counts = lax.dynamic_index_in_dim(block_rows, slot, 0, keepdims=False)
    live = lax.dynamic_index_in_dim(slot_live, slot, 0, keepdims=False) > 0
    within = jnp.arange(block_len, dtype=jnp.int32)
    key_valid = (within[None, :] < counts[:, None]) & live
    key_bias = jnp.where(key_valid, 0.0, MASKED).astype(F32).reshape(-1, 1)
    row_mask = (
        ((within < lax.dynamic_index_in_dim(counts, ctx, 0, keepdims=False)) & live)
        .astype(F32)[:, None]
    )

    source = lax.dynamic_index_in_dim(tokens, slot, 0, keepdims=False).astype(F32)
    normal_one, inverse_one = layer_stats(source)
    normed = (normal_one * ln1_gain + ln1_bias).astype(BF16)
    shifts = [
        [biases[h][:half_qv] for h in range(2)],
        None,
        [biases[h][half_qv : 2 * half_qv] for h in range(2)],
    ]
    mixed = []
    for c in range(3):
        columns = []
        for h in range(2):
            value = dot(normed, full_qkv[c][h], 1, 0)
            columns.append((value if shifts[c] is None else value + shifts[c][h]).astype(BF16))
        mixed.append(split_heads(columns))
    sent = jnp.stack([jnp.stack([mixed[c][j] for c in range(3)]) for j in range(RING)])
    heads = exchange(sent)
    queries, keys, values = (heads[:, c].reshape(RING * block_len, 128) for c in range(3))
    mixed_values, logs = attend(queries, keys, values, key_bias)
    attended = join_heads(exchange(mixed_values.reshape(RING, block_len, 128)))
    attn_part = dot(attended[0], full_proj[0], 1, 1) + dot(attended[1], full_proj[1], 1, 1)
    branch_attn = pair_sum(attn_part) + b_proj
    middle = source + scale_attn * branch_attn

    normal_two, inverse_two = layer_stats(middle)
    second = (normal_two * ln2_gain + ln2_bias).astype(BF16)
    grad_out = row_mask * lax.dynamic_index_in_dim(cotangent, slot, 0, keepdims=False).astype(F32)
    grad_branch_mlp = (grad_out * scale_mlp).astype(BF16)
    grad_b_down = jnp.sum(grad_branch_mlp.astype(F32), axis=0)
    active, grad_hidden, mlp_part, second_part, grad_b_up = feed_forward_both_ways(
        second,
        grad_branch_mlp,
        others,
        jnp.concatenate([biases[h][2 * half_qv :] for h in range(2)]).reshape(-1, 1, 256),
    )
    grad_second = pair_sum(second_part)
    branch_mlp = pair_sum(mlp_part) + b_down
    result_here = (row_mask * (middle + scale_mlp * branch_mlp)).astype(BF16)
    grad_scale_mlp = jnp.sum(grad_out * branch_mlp, axis=0)

    grad_ln2_gain = jnp.sum(grad_second * normal_two, axis=0)
    grad_ln2_bias = jnp.sum(grad_second, axis=0)
    grad_middle = grad_out + norm_back(grad_second * ln2_gain, normal_two, inverse_two)
    grad_scale_attn = jnp.sum(grad_middle * branch_attn, axis=0)
    grad_branch = (grad_middle * scale_attn).astype(BF16)
    grad_b_proj = jnp.sum(grad_branch.astype(F32), axis=0)
    grad_attended = [dot(grad_branch, full_proj[h], 1, 0).astype(BF16) for h in range(2)]
    grad_heads = exchange(jnp.stack(split_heads(grad_attended))).reshape(RING * block_len, 128)
    joined = joined_gradients(
        (second.T, grad_branch_mlp.T, grad_branch.T),
        (grad_hidden, active, jnp.concatenate(attended, axis=1)),
    )
    joined = lax.psum_scatter(joined, ("z", "x"), scatter_dimension=0, tiled=True)
    three = attend_back(queries, keys, values, grad_heads, key_bias, logs)
    returned = exchange(
        jnp.stack([value.reshape(RING, block_len, 128) for value in three], axis=1)
    )
    chunk = w_up.shape[0]
    grad_w_qkv, normed_part, sums_qkv = qkv_gradients(normed.T, returned, full_qkv, chunk)
    grad_normed = pair_sum(normed_part)
    grad_ln1_gain = jnp.sum(grad_normed * normal_one, axis=0)
    grad_ln1_bias = jnp.sum(grad_normed, axis=0)
    tokens_here = grad_middle + norm_back(grad_normed * ln1_gain, normal_one, inverse_one)
    grad_w_qkv = lax.all_to_all(
        grad_w_qkv.reshape(-1, 256),
        ("y_hi", "y_lo", "z", "x"),
        split_axis=0,
        concat_axis=0,
        tiled=True,
    )
    w_qkv_here = jnp.sum(grad_w_qkv.reshape(-1, 3, chunk, half_qv).astype(F32), axis=0).swapaxes(0, 1)
    grad_b_qv = [
        jnp.concatenate([sums_qkv[2 * h, c], sums_qkv[2 * h + 1, c]]) for h in range(2) for c in (0, 2)
    ]

    width = joined.shape[1] // 2
    joined = joined.reshape(2 * chunk, 2, width).swapaxes(0, 1).reshape(RING, 1, 1, chunk, width)
    joined = scatter_axis(joined, "y", at, way).reshape(chunk, width)
    w_up_here, w_down_here, w_proj_here = jnp.split(joined, cuts, axis=1)
    wide = [
        grad_ln1_gain,
        grad_ln1_bias,
        grad_b_proj,
        grad_scale_attn,
        grad_ln2_gain,
        grad_ln2_bias,
        grad_b_down,
        grad_scale_mlp,
    ]
    vector = jnp.concatenate(wide + grad_b_qv + [grad_b_up.reshape(-1)])
    vector = sum_everywhere(vector.reshape(-1, 128)).reshape(-1)
    width = tokens.shape[2]
    sums = [vector[i * width : (i + 1) * width] for i in range(len(wide))]
    rest = vector[len(wide) * width :]
    qv_here = lax.dynamic_slice_in_dim(rest, slot * 2 * half_qv, 2 * half_qv, 0).reshape(2, half_qv)
    up_len = b_up.shape[0]
    up_here = lax.dynamic_slice_in_dim(rest, 4 * half_qv + slot * up_len, up_len, 0)
    result = both_slots(result_here, slot, core)
    d_tokens = both_slots(tokens_here.astype(BF16), slot, core).astype(F32)
    return (
        result,
        d_tokens,
        sums[0],
        sums[1],
        w_qkv_here,
        qv_here,
        w_proj_here,
        sums[2],
        sums[3],
        sums[4],
        sums[5],
        w_up_here,
        up_here,
        w_down_here,
        sums[6],
        sums[7],
    )


def solution(mesh):
    torus = jax.sharding.Mesh(
        mesh.devices.reshape([size for _, size in AXES]), [name for name, _ in AXES]
    )
    shard, rows, pair = ("y_lo", "z"), ("y_lo", "z", "x"), ("y_hi", "core")
    matrix = P(rows, pair)
    images = P(shard, "x", None)
    w_qkv = P(rows, None, pair)
    return jax.shard_map(
        per_device,
        mesh=torus,
        in_specs=(
            images,
            images,
            P(shard),
            P(shard, None),
            P(),
            P(),
            w_qkv,
            P(None, pair),
            matrix,
            P(),
            P(),
            P(),
            P(),
            matrix,
            P(pair),
            matrix,
            P(),
            P(),
        ),
        out_specs=(
            images,
            images,
            P(),
            P(),
            w_qkv,
            P(None, pair),
            matrix,
            P(),
            P(),
            P(),
            P(),
            matrix,
            P(pair),
            matrix,
            P(),
            P(),
        ),
        check_vma=False,
    )
```

```python
import jax
import jax.numpy as jnp
from jax import lax
from jax.experimental import pallas as pl
from jax.experimental.pallas import tpu as pltpu
from jax.sharding import PartitionSpec as P

HEAD_DIM = 64
EPSILON = 1e-06
MASKED = -1e30
RING = 4
BF16 = jnp.bfloat16
F32 = jnp.float32

AXES = (("y_lo", 2), ("z", RING), ("x", RING), ("y_hi", 2), ("core", 2))
DIM = {"y": 0, "z": 1, "x": 2}
ORDERS = (("z", "y", "x"), ("x", "z", "y"), ("y", "x", "z"))


def step_ring(value, axis, step):
    names = ("y_lo", "y_hi", "core") if axis == "y" else (axis, "core")
    place = (lambda p: (p % 2) * 2 + p // 2) if axis == "y" else (lambda p: p)
    pairs = [
        (place(p) * 2 + core, place((p + (-step if core else step)) % RING) * 2 + core)
        for p in range(RING)
        for core in range(2)
    ]
    return lax.ppermute(value, names, pairs)


def swap(value, axis, bit=1):
    return lax.ppermute(value, axis, [(i, i ^ bit) for i in range(lax.axis_size(axis))])


def positions():
    return {
        "x": lax.axis_index("x"),
        "z": lax.axis_index("z"),
        "y": 2 * lax.axis_index("y_hi") + lax.axis_index("y_lo"),
    }


def gather_axis(value, axis, at, way):
    dim = DIM[axis]
    size = value.shape[dim]
    behind = step_ring(value, axis, 1)
    two = step_ring(jnp.concatenate([value, behind], dim), axis, 2)
    parts = [value, behind] + [lax.slice_in_dim(two, i * size, (i + 1) * size, axis=dim) for i in (0, 1)]
    shape = list(value.shape)
    shape[dim] *= RING
    out = jnp.zeros(shape, value.dtype)
    for step, part in enumerate(parts):
        out = lax.dynamic_update_slice_in_dim(out, part, ((at[axis] - step * way) % RING) * size, dim)
    return out


def gather(chunk, order, at, way):
    value = chunk[None, None, None]
    for axis in order:
        value = gather_axis(value, axis, at, way)
    return value.reshape(2, RING * RING * 2 * chunk.shape[0], chunk.shape[1])


def scatter_axis(value, axis, at, way):
    dim = DIM[axis]

    def block(step):
        return lax.dynamic_slice_in_dim(value, (at[axis] + step * way) % RING, 1, dim)

    far = step_ring(jnp.concatenate([block(2), block(3)], dim), axis, 2)
    here, next_one = (lax.slice_in_dim(far, i, i + 1, axis=dim).astype(F32) for i in (0, 1))
    near = step_ring((block(1).astype(F32) + next_one).astype(BF16), axis, 1)
    return block(0).astype(F32) + here + near.astype(F32)


def sum_everywhere(vector, beside):
    for place, (axis, bit) in enumerate(
        (("x", 1), ("x", 2), ("z", 1), ("z", 2), ("y_lo", 1), ("y_hi", 1))
    ):
        if place == 2:
            vector, beside = lax.optimization_barrier((vector, beside))
        vector = vector + swap(vector, axis, bit)
    return vector, beside


def exchange(blocks):
    return lax.all_to_all(blocks, "x", split_axis=0, concat_axis=0, tiled=True)


def layer_stats(values):
    average = jnp.mean(values, axis=-1, keepdims=True)
    centered = values - average
    variance = jnp.mean(centered * centered, axis=-1, keepdims=True)
    inverse = lax.rsqrt(variance + EPSILON)
    return (centered * inverse, inverse)


def norm_back(grad_hat, normal_hat, inverse):
    first_term = jnp.mean(grad_hat, axis=-1, keepdims=True)
    second_term = jnp.mean(grad_hat * normal_hat, axis=-1, keepdims=True)
    return inverse * (grad_hat - first_term - normal_hat * second_term)


def dot(left, right, left_dim, right_dim):
    return lax.dot_general(
        left, right, (((left_dim,), (right_dim,)), ((), ())), preferred_element_type=F32
    )


def pair_sum(part):
    low = part.astype(BF16)
    return low.astype(F32) + swap(low, "core").astype(F32)


def head_lanes(head, width):
    lanes = lax.broadcasted_iota(jnp.int32, (1, width), 1) // HEAD_DIM
    return jnp.where(lanes == head, 1.0, 0.0).astype(F32)


def attention_forward(q_ref, k_ref, v_ref, bias_ref, out_ref, log_ref, out_total):
    out_total[...] = jnp.zeros_like(out_total)

    @pl.loop(0, 2)
    def _(head):
        here = head_lanes(head, q_ref.shape[1])
        scaled = q_ref[...] * (here * HEAD_DIM ** (-0.5)).astype(BF16)
        scores = dot(k_ref[...], scaled, 1, 1) + bias_ref[...]
        top = jnp.max(scores, axis=0, keepdims=True)
        powers = jnp.exp(scores - top)
        total = jnp.sum(powers, axis=0, keepdims=True)
        weights = (powers * (1.0 / total)).astype(BF16)
        mixed = dot(v_ref[...], weights, 0, 0)
        out_total[...] += mixed.T * here
        log_ref[0, pl.ds(head, 1), :] = top + jnp.log(total)

    out_ref[...] = out_total[...].astype(BF16)


def attention_backward(
    q_ref, k_ref, v_ref, g_ref, bias_ref, log_ref, dq_ref, dk_ref, dv_ref, dq_total, dk_total, dv_total
):
    step = pl.program_id(0)

    @pl.when(step == 0)
    def _():
        dk_total[...] = jnp.zeros_like(dk_total)
        dv_total[...] = jnp.zeros_like(dv_total)

    dq_total[...] = jnp.zeros_like(dq_total)

    @pl.loop(0, 2)
    def _(head):
        here = head_lanes(head, q_ref.shape[1])
        scaled = q_ref[...] * (here * HEAD_DIM ** (-0.5)).astype(BF16)
        grad = g_ref[...] * here.astype(BF16)
        scores = dot(k_ref[...], scaled, 1, 1) + bias_ref[...]
        probs = jnp.exp(scores - log_ref[0, pl.ds(head, 1), :])
        grad_probs = dot(v_ref[...], grad, 1, 1)
        row_dot = jnp.sum(probs * grad_probs, axis=0, keepdims=True)
        grad_scores = (probs * (grad_probs - row_dot)).astype(BF16)
        dq_total[...] += dot(k_ref[...], grad_scores, 0, 0).T * (here * HEAD_DIM ** (-0.5))
        dk_total[...] += dot(grad_scores, scaled, 1, 0)
        dv_total[...] += dot(probs.astype(BF16), grad, 1, 0)

    dq_ref[...] = dq_total[...].astype(BF16)

    @pl.when(step == pl.num_programs(0) - 1)
    def _():
        dk_ref[...] = dk_total[...].astype(BF16)
        dv_ref[...] = dv_total[...].astype(BF16)


def attend(queries, keys, values, bias):
    rows, width = queries.shape
    block = rows // RING
    part = pl.BlockSpec((block, width), lambda i: (i, 0))
    whole = pl.BlockSpec((rows, width), lambda i: (0, 0))
    log_spec = pl.BlockSpec((1, 2, block), lambda i: (i, 0, 0))
    return pl.pallas_call(
        attention_forward,
        grid=(RING,),
        in_specs=[part, whole, whole, pl.BlockSpec((rows, 1), lambda i: (0, 0))],
        out_specs=[part, log_spec],
        out_shape=[
            jax.ShapeDtypeStruct((rows, width), BF16),
            jax.ShapeDtypeStruct((RING, 2, block), F32),
        ],
        scratch_shapes=[pltpu.VMEM((block, width), F32)],
        compiler_params=pltpu.CompilerParams(vmem_limit_bytes=40 << 20),
        cost_estimate=pl.CostEstimate(
            flops=4 * rows * rows * width, bytes_accessed=8 * rows * width, transcendentals=2 * rows * rows
        ),
    )(queries, keys, values, bias)


def attend_back(queries, keys, values, grad, bias, logs):
    rows, width = queries.shape
    block = rows // RING
    part = pl.BlockSpec((block, width), lambda i: (i, 0))
    whole = pl.BlockSpec((rows, width), lambda i: (0, 0))
    log_spec = pl.BlockSpec((1, 2, block), lambda i: (i, 0, 0))
    return pl.pallas_call(
        attention_backward,
        grid=(RING,),
        in_specs=[part, whole, whole, part, pl.BlockSpec((rows, 1), lambda i: (0, 0)), log_spec],
        out_specs=[part, whole, whole],
        out_shape=[jax.ShapeDtypeStruct((rows, width), BF16)] * 3,
        scratch_shapes=[pltpu.VMEM((block, width), F32)] + [pltpu.VMEM((rows, width), F32)] * 2,
        compiler_params=pltpu.CompilerParams(vmem_limit_bytes=40 << 20),
        cost_estimate=pl.CostEstimate(
            flops=10 * rows * rows * width, bytes_accessed=14 * rows * width, transcendentals=2 * rows * rows
        ),
    )(queries, keys, values, grad, bias, logs)


def feed_forward(
    x_ref, g_ref, up_ref, down_ref, bias_ref, act_ref, hid_ref, out_ref, back_ref, sum_ref, out_total, back_total
):
    step = pl.program_id(0)

    @pl.when(step == 0)
    def _():
        out_total[...] = jnp.zeros_like(out_total)
        back_total[...] = jnp.zeros_like(back_total)

    up, down = up_ref[0], down_ref[0]
    hidden = dot(x_ref[...], up, 1, 0) + bias_ref[0]
    below = 0.5 * (1.0 + lax.erf(hidden * 0.7071067811865476))
    slope = below + hidden * (jnp.exp(-0.5 * hidden * hidden) * 0.3989422804014327)
    active = (hidden * below).astype(BF16)
    grad_hidden = (dot(g_ref[...], down, 1, 0) * slope).astype(BF16)
    act_ref[...] = active
    hid_ref[...] = grad_hidden
    sum_ref[0] = jnp.sum(grad_hidden.astype(F32), axis=0, keepdims=True)
    out_total[...] += dot(active, down, 1, 1)
    back_total[...] += dot(grad_hidden, up, 1, 1)

    @pl.when(step == pl.num_programs(0) - 1)
    def _():
        out_ref[...] = out_total[...].astype(BF16)
        back_ref[...] = back_total[...].astype(BF16)


def feed_forward_both_ways(second, grad, weights, bias):
    rows, width = second.shape
    steps = bias.shape[0]
    half = steps // 2
    whole = pl.BlockSpec((rows, width), lambda j: (0, 0))
    part = pl.BlockSpec((rows, 256), lambda j: (0, j))
    small = pl.BlockSpec((1, 1, 256), lambda j: (j, 0, 0))
    return pl.pallas_call(
        feed_forward,
        grid=(steps,),
        in_specs=[
            whole,
            whole,
            pl.BlockSpec((1, width, 256), lambda j: (j // half, 0, j % half)),
            pl.BlockSpec((1, width, 256), lambda j: (j // half, 0, half + j % half)),
            small,
        ],
        out_specs=[part, part, whole, whole, small],
        out_shape=[jax.ShapeDtypeStruct((rows, 256 * steps), BF16)] * 2
        + [jax.ShapeDtypeStruct((rows, width), BF16)] * 2
        + [jax.ShapeDtypeStruct((steps, 1, 256), F32)],
        scratch_shapes=[pltpu.VMEM((rows, width), F32)] * 2,
        compiler_params=pltpu.CompilerParams(vmem_limit_bytes=40 << 20),
        cost_estimate=pl.CostEstimate(
            flops=8 * rows * width * 256 * steps,
            bytes_accessed=4 * width * 256 * steps,
            transcendentals=2 * rows * 256 * steps,
        ),
    )(second, grad, weights, weights, bias)


def joined_gradient(
    second_ref, mlp_ref, attn_ref, hid_ref, act_ref, att_ref, out_ref, second_turned, mlp_turned, attn_turned
):
    block = pl.program_id(0) % 9

    @pl.when(pl.program_id(0) == 0)
    def _():
        second_turned[...] = second_ref[...].T
        mlp_turned[...] = mlp_ref[...].T
        attn_turned[...] = attn_ref[...].T

    def write(left_ref, right_ref):
        value = dot(left_ref[...], right_ref[...], 1, 0).astype(BF16)
        chunk = value.shape[0] // (2 * RING * RING)
        for y_lo in range(2):
            for place in range(RING * RING):
                rows = value[(y_lo * RING * RING + place) * chunk :][:chunk]
                out_ref[pl.ds((place * 2 + y_lo) * chunk, chunk), :] = rows

    @pl.when(block < 4)
    def _():
        write(second_turned, hid_ref)

    @pl.when((block >= 4) & (block < 8))
    def _():
        write(mlp_turned, act_ref)

    @pl.when(block == 8)
    def _():
        write(attn_turned, att_ref)


def gradient_cost(rows, depth, columns):
    return pl.CostEstimate(
        flops=2 * rows * depth * columns, bytes_accessed=2 * rows * columns, transcendentals=0
    )


def joined_gradients(lefts, rights):
    depth, rows = lefts[0].shape
    columns = sum(right.shape[1] for right in rights)
    whole = pl.BlockSpec((depth, rows), lambda j: (0, 0))
    return pl.pallas_call(
        joined_gradient,
        grid=(columns // 256,),
        in_specs=[
            whole,
            whole,
            whole,
            pl.BlockSpec((depth, 256), lambda j: (0, j // 9 * 4 + jnp.minimum(j % 9, 3))),
            pl.BlockSpec((depth, 256), lambda j: (0, j // 9 * 4 + jnp.clip(j % 9 - 4, 0, 3))),
            pl.BlockSpec((depth, 256), lambda j: (0, j // 9)),
        ],
        out_specs=pl.BlockSpec((rows, 256), lambda j: (0, j)),
        out_shape=jax.ShapeDtypeStruct((rows, columns), BF16),
        scratch_shapes=[pltpu.VMEM((rows, depth), BF16)] * 3,
        compiler_params=pltpu.CompilerParams(vmem_limit_bytes=40 << 20),
        cost_estimate=gradient_cost(rows, depth, columns),
    )(*lefts, *rights)


def qkv_gradient(left_ref, grad_ref, q_ref, k_ref, v_ref, out_ref, back_ref, sum_ref, back_total, turned):
    step = pl.program_id(0)

    @pl.when(step == 0)
    def _():
        back_total[...] = jnp.zeros_like(back_total)
        turned[...] = left_ref[...].T

    for c, weights in enumerate((q_ref, k_ref, v_ref)):
        grad = grad_ref[0, c]
        value = dot(turned[...], grad, 1, 0).astype(BF16)
        out_ref[0, :, c] = value.reshape(out_ref.shape[1], out_ref.shape[3], out_ref.shape[4])
        back_total[...] += dot(grad, weights[0], 1, 1)
        sum_ref[0, c : c + 1, :] = jnp.sum(grad.astype(F32), axis=0, keepdims=True)

    @pl.when(step == pl.num_programs(0) - 1)
    def _():
        back_ref[...] = back_total[...].astype(BF16)


def qkv_gradients(left, grads, weights, chunk):
    rows, width = left.shape
    weight = pl.BlockSpec((1, width, 128), lambda j: (j // 2, 0, j % 2))
    return pl.pallas_call(
        qkv_gradient,
        grid=(RING,),
        in_specs=[
            pl.BlockSpec((rows, width), lambda j: (0, 0)),
            pl.BlockSpec((1, 3, rows, 128), lambda j: (j, 0, 0, 0)),
            weight,
            weight,
            weight,
        ],
        out_specs=[
            pl.BlockSpec((1, width // chunk, 3, chunk, 128), lambda j: (j // 2, 0, 0, 0, j % 2)),
            pl.BlockSpec((rows, width), lambda j: (0, 0)),
            pl.BlockSpec((1, 3, 128), lambda j: (j, 0, 0)),
        ],
        out_shape=[
            jax.ShapeDtypeStruct((2, width // chunk, 3, chunk, 256), BF16),
            jax.ShapeDtypeStruct((rows, width), BF16),
            jax.ShapeDtypeStruct((RING, 3, 128), F32),
        ],
        scratch_shapes=[pltpu.VMEM((rows, width), F32), pltpu.VMEM((width, rows), BF16)],
        compiler_params=pltpu.CompilerParams(vmem_limit_bytes=40 << 20),
        cost_estimate=gradient_cost(2 * width, rows, 12 * 128),
    )(left, grads, *weights)


def split_heads(blocks):
    return [blocks[j // 2][:, (j % 2) * 128 : (j % 2) * 128 + 128] for j in range(RING)]


def join_heads(four):
    return [jnp.concatenate([four[2 * h], four[2 * h + 1]], axis=1) for h in range(2)]


def both_slots(value, slot, core):
    half = value.shape[0] // 2
    sent = lax.dynamic_slice_in_dim(value, core * half, half, 0)
    mine = swap(sent, "y_hi")
    other = swap(mine, "core")
    first, last = jnp.where(core == 0, mine, other), jnp.where(core == 0, other, mine)
    far = jnp.concatenate([first, last], axis=0)
    return jnp.stack([jnp.where(slot == 0, value, far), jnp.where(slot == 0, far, value)])


def per_device(
    tokens,
    cotangent,
    slot_live,
    block_rows,
    ln1_gain,
    ln1_bias,
    w_qkv,
    b_qv,
    w_proj,
    b_proj,
    scale_attn,
    ln2_gain,
    ln2_bias,
    w_up,
    b_up,
    w_down,
    b_down,
    scale_mlp,
):
    block_len = tokens.shape[1]
    at = positions()
    slot, core = lax.axis_index("y_hi"), lax.axis_index("core")
    ctx = at["x"]
    way = 1 - 2 * core

    cuts = (w_up.shape[1], w_up.shape[1] + w_down.shape[1])
    others = lax.all_gather(
        jnp.concatenate([w_up, w_down, w_proj], axis=1), ("y_hi", "y_lo", "z", "x"), axis=0, tiled=True
    )
    others = others.reshape(2, -1, others.shape[1])
    full_proj = [others[h, :, cuts[1] :] for h in range(2)]
    full_qkv = [gather(w_qkv[:, c], ORDERS[c], at, way) for c in range(3)]
    biases = jnp.concatenate([b_qv.reshape(-1), b_up])
    other_biases = swap(biases, "y_hi")
    biases = [jnp.where(slot == h, biases, other_biases) for h in range(2)]
    half_qv = b_qv.shape[1]

    counts = lax.dynamic_index_in_dim(block_rows, slot, 0, keepdims=False)
    live = lax.dynamic_index_in_dim(slot_live, slot, 0, keepdims=False) > 0
    within = jnp.arange(block_len, dtype=jnp.int32)
    key_valid = (within[None, :] < counts[:, None]) & live
    key_bias = jnp.where(key_valid, 0.0, MASKED).astype(F32).reshape(-1, 1)
    row_mask = (
        ((within < lax.dynamic_index_in_dim(counts, ctx, 0, keepdims=False)) & live)
        .astype(F32)[:, None]
    )

    source = lax.dynamic_index_in_dim(tokens, slot, 0, keepdims=False).astype(F32)
    normal_one, inverse_one = layer_stats(source)
    normed = (normal_one * ln1_gain + ln1_bias).astype(BF16)
    shifts = [
        [biases[h][:half_qv] for h in range(2)],
        None,
        [biases[h][half_qv : 2 * half_qv] for h in range(2)],
    ]
    mixed = []
    for c in range(3):
        columns = []
        for h in range(2):
            value = dot(normed, full_qkv[c][h], 1, 0)
            columns.append((value if shifts[c] is None else value + shifts[c][h]).astype(BF16))
        mixed.append(split_heads(columns))
    sent = jnp.stack([jnp.stack([mixed[c][j] for c in range(3)]) for j in range(RING)])
    heads = exchange(sent)
    queries, keys, values = (heads[:, c].reshape(RING * block_len, 128) for c in range(3))
    mixed_values, logs = attend(queries, keys, values, key_bias)
    attended = join_heads(exchange(mixed_values.reshape(RING, block_len, 128)))
    attn_part = dot(attended[0], full_proj[0], 1, 1) + dot(attended[1], full_proj[1], 1, 1)
    branch_attn = pair_sum(attn_part) + b_proj
    middle = source + scale_attn * branch_attn

    normal_two, inverse_two = layer_stats(middle)
    second = (normal_two * ln2_gain + ln2_bias).astype(BF16)
    grad_out = row_mask * lax.dynamic_index_in_dim(cotangent, slot, 0, keepdims=False).astype(F32)
    grad_branch_mlp = (grad_out * scale_mlp).astype(BF16)
    grad_b_down = jnp.sum(grad_branch_mlp.astype(F32), axis=0)
    active, grad_hidden, mlp_part, second_part, grad_b_up = feed_forward_both_ways(
        second,
        grad_branch_mlp,
        others,
        jnp.concatenate([biases[h][2 * half_qv :] for h in range(2)]).reshape(-1, 1, 256),
    )
    grad_second = pair_sum(second_part)
    branch_mlp = pair_sum(mlp_part) + b_down
    result_here = (row_mask * (middle + scale_mlp * branch_mlp)).astype(BF16)
    grad_scale_mlp = jnp.sum(grad_out * branch_mlp, axis=0)

    grad_ln2_gain = jnp.sum(grad_second * normal_two, axis=0)
    grad_ln2_bias = jnp.sum(grad_second, axis=0)
    grad_middle = grad_out + norm_back(grad_second * ln2_gain, normal_two, inverse_two)
    grad_scale_attn = jnp.sum(grad_middle * branch_attn, axis=0)
    grad_branch = (grad_middle * scale_attn).astype(BF16)
    grad_b_proj = jnp.sum(grad_branch.astype(F32), axis=0)
    grad_attended = [dot(grad_branch, full_proj[h], 1, 0).astype(BF16) for h in range(2)]
    grad_heads = exchange(jnp.stack(split_heads(grad_attended))).reshape(RING * block_len, 128)
    joined = joined_gradients(
        (second, grad_branch_mlp, grad_branch),
        (grad_hidden, active, jnp.concatenate(attended, axis=1)),
    )
    joined = lax.psum_scatter(joined, ("z", "x"), scatter_dimension=0, tiled=True)
    three = attend_back(queries, keys, values, grad_heads, key_bias, logs)
    returned = exchange(
        jnp.stack([value.reshape(RING, block_len, 128) for value in three], axis=1)
    )
    chunk = w_up.shape[0]
    grad_w_qkv, normed_part, sums_qkv = qkv_gradients(normed, returned, full_qkv, chunk)
    grad_normed = pair_sum(normed_part)
    grad_ln1_gain = jnp.sum(grad_normed * normal_one, axis=0)
    grad_ln1_bias = jnp.sum(grad_normed, axis=0)
    tokens_here = grad_middle + norm_back(grad_normed * ln1_gain, normal_one, inverse_one)
    grad_w_qkv = lax.all_to_all(
        grad_w_qkv.reshape(-1, 256),
        ("y_hi", "y_lo", "z", "x"),
        split_axis=0,
        concat_axis=0,
        tiled=True,
    )
    w_qkv_here = jnp.sum(grad_w_qkv.reshape(-1, 3, chunk, half_qv).astype(F32), axis=0).swapaxes(0, 1)
    grad_b_qv = [
        jnp.concatenate([sums_qkv[2 * h, c], sums_qkv[2 * h + 1, c]]) for h in range(2) for c in (0, 2)
    ]

    width = joined.shape[1] // 2
    joined = joined.reshape(2 * chunk, 2, width).swapaxes(0, 1).reshape(RING, 1, 1, chunk, width)
    joined = scatter_axis(joined, "y", at, way).reshape(chunk, width)
    wide = [
        grad_ln1_gain,
        grad_ln1_bias,
        grad_b_proj,
        grad_scale_attn,
        grad_ln2_gain,
        grad_ln2_bias,
        grad_b_down,
        grad_scale_mlp,
    ]
    vector = jnp.concatenate(wide + grad_b_qv + [grad_b_up.reshape(-1)])
    vector, joined = sum_everywhere(vector.reshape(-1, 128), joined)
    vector = vector.reshape(-1)
    w_up_here, w_down_here, w_proj_here = jnp.split(joined, cuts, axis=1)
    width = tokens.shape[2]
    sums = [vector[i * width : (i + 1) * width] for i in range(len(wide))]
    rest = vector[len(wide) * width :]
    qv_here = lax.dynamic_slice_in_dim(rest, slot * 2 * half_qv, 2 * half_qv, 0).reshape(2, half_qv)
    up_len = b_up.shape[0]
    up_here = lax.dynamic_slice_in_dim(rest, 4 * half_qv + slot * up_len, up_len, 0)
    result = both_slots(result_here, slot, core)
    d_tokens = both_slots(tokens_here.astype(BF16), slot, core).astype(F32)
    return (
        result,
        d_tokens,
        sums[0],
        sums[1],
        w_qkv_here,
        qv_here,
        w_proj_here,
        sums[2],
        sums[3],
        sums[4],
        sums[5],
        w_up_here,
        up_here,
        w_down_here,
        sums[6],
        sums[7],
    )


def solution(mesh):
    torus = jax.sharding.Mesh(
        mesh.devices.reshape([size for _, size in AXES]), [name for name, _ in AXES]
    )
    shard, rows, pair = ("y_lo", "z"), ("y_lo", "z", "x"), ("y_hi", "core")
    matrix = P(rows, pair)
    images = P(shard, "x", None)
    w_qkv = P(rows, None, pair)
    return jax.shard_map(
        per_device,
        mesh=torus,
        in_specs=(
            images,
            images,
            P(shard),
            P(shard, None),
            P(),
            P(),
            w_qkv,
            P(None, pair),
            matrix,
            P(),
            P(),
            P(),
            P(),
            matrix,
            P(pair),
            matrix,
            P(),
            P(),
        ),
        out_specs=(
            images,
            images,
            P(),
            P(),
            w_qkv,
            P(None, pair),
            matrix,
            P(),
            P(),
            P(),
            P(),
            matrix,
            P(pair),
            matrix,
            P(),
            P(),
        ),
        check_vma=False,
    )
```
